128 devices in a mesh: gx: 16 (over x, y), gy: 8 (over z, core).
Axes of the slice: x: 4, y: 4, z: 4, core: 2. Of those that a mesh axis runs over, the one named last changes fastest.
Arguments:
- efield_vector: float32 [3, 512, 256, 256], P(None, 'gx', 'gy'), may hold values from -6 to 6
- hfield_vector: float32 [3, 512, 256, 256], P(None, 'gx', 'gy'), may hold values from -6 to 6
- dielectric_grid: float32 [512, 256, 256], P('gx', 'gy'), may hold values from 1 to 6
- sigma_grid: float32 [512, 256, 256], P('gx', 'gy'), may hold values from 0 to 0.5
- substance_label: int32 [512, 256, 256], P('gx', 'gy'), may hold values from 0 to 2
- thermal_state: float32 [16384, 8, 256], P(('gx', 'gy')), may hold values from 0 to 2
- wetness_share: float32 [16384, 8, 256], P(('gx', 'gy')), may hold values from 0.1 to 1
- dielectric_line_choice: int32 [16384, 8, 256], P(('gx', 'gy')), may hold values from 0 to 15
- dielectric_lookup_lines: float32 [4, 16], replicated, may hold values from 0.2 to 2
- dispatch_keeper_map: int32 [128, 128], P(('gx', 'gy')), may hold values from 0 to 127, each once within a row
- arrival_position_map: int32 [128, 128], P(('gx', 'gy')), may hold values from 0 to 127, each once within a row
Outputs:
- final_efield: float32 [3, 512, 256, 256], P(None, 'gx', 'gy')
- final_hfield: float32 [3, 512, 256, 256], P(None, 'gx', 'gy')
- permittivity_out: float32 [512, 256, 256], P('gx', 'gy')
- conductivity_out: float32 [512, 256, 256], P('gx', 'gy')
- temperature_out: float32 [16384, 8, 256], P(('gx', 'gy'))
- moisture_out: float32 [16384, 8, 256], P(('gx', 'gy'))
The draws below stay inside these ranges and needn't reach their ends.
Inputs may be any that keep to these rules, and one draw needn't show every extreme that they name: Each row names every device index once: block k of device s goes to device dispatch_keeper_map[s, k]. `arrival_position_map`: each row names every slot once.
All inputs are finite; a program needn't handle non-finite values.
Results may differ from the reference program's by a relative error of at most 0.00002.
Values sent between devices are 32-bit elements; how exact they have to be, the bound alone decides.
No kernel may reach another device: no remote copies, remote signals or barrier semaphores. Data moves between devices by JAX's collectives and lax.ppermute only.
A program may use at most 128 MiB of HBM per device.

```python
import jax
import jax.numpy as jnp
from jax import lax

CX = 32
CY = 32
CAVITY_DEPTH = 256
STEPS = 2
LEVELS = 16
X = 512
Y = 256
TILE_DEPTH_LINES = 8
TILE_COUNT = 16384
N_GX = 16
N_GY = 8
DEVICES = 128


def plant(result, rng, smallest, largest):
    place = [jax.random.randint(jax.random.fold_in(rng, axis), (), 0, length) for axis, length in enumerate(result.shape)]
    widest = result.shape.index(max(result.shape))
    beside = place[:widest] + [(place[widest] + 1) % result.shape[widest]] + place[widest + 1:]
    return result.at[tuple(place)].set(smallest).at[tuple(beside)].set(largest)


def steps_of(own_key, shape, shards, low, top_value):
    def one(dim, parts):
        heights = jax.random.uniform(jax.random.fold_in(jax.random.fold_in(own_key, 6), dim), (parts,), jnp.float32, low / len(shards), top_value / len(shards))
        return jnp.repeat(jnp.exp(heights), shape[dim] // parts).reshape((-1,) + (1,) * (len(shape) - dim - 1))

    loudness = one(*shards[0])
    for cut in shards[1:]:
        loudness = loudness * one(*cut)
    return loudness


def normal_values(own_key, dims, width, most, shards=(), dtype=jnp.bfloat16):
    factor_of = steps_of(own_key, dims, shards, -0.22, 0.18) if shards else 1.0
    result = jax.random.normal(own_key, dims, jnp.float32) * width * factor_of
    return jnp.minimum(jnp.maximum(result, -most), most).astype(dtype)


def setup_inputs(seed: int = 0) -> dict:
    key_list = jax.random.split(jax.random.key(seed), 12)
    efield_vector = normal_values(key_list[0], (3, X, Y, CAVITY_DEPTH), 1.0, 6.0, ((1, 16), (2, 8)), jnp.float32)
    hfield_vector = normal_values(key_list[1], (3, X, Y, CAVITY_DEPTH), 1.0, 6.0, ((1, 16), (2, 8)), jnp.float32)
    dielectric_grid = jnp.clip(1.0 + 5.0 * jax.random.uniform(key_list[2], (X, Y, CAVITY_DEPTH), jnp.float32) ** steps_of(key_list[2], (X, Y, CAVITY_DEPTH), ((0, 16), (1, 8)), -0.2, 0.2), 1.0, 6.0)
    sigma_grid = jnp.clip(0.5 * jax.random.uniform(key_list[3], (X, Y, CAVITY_DEPTH), jnp.float32) ** steps_of(key_list[3], (X, Y, CAVITY_DEPTH), ((0, 16), (1, 8)), -0.2, 0.2), 0.0, 0.5)
    substance_label = plant(jax.random.randint(key_list[4], (X, Y, CAVITY_DEPTH), 0, 3), jax.random.fold_in(key_list[4], 1), 0, 2).astype(jnp.int32)
    thermal_state = jnp.clip(2.0 * jax.random.uniform(key_list[5], (TILE_COUNT, TILE_DEPTH_LINES, CAVITY_DEPTH), jnp.float32) ** steps_of(key_list[5], (TILE_COUNT, TILE_DEPTH_LINES, CAVITY_DEPTH), ((0, 128),), -0.2, 0.2), 0.0, 2.0)
    wetness_share = jnp.clip(0.1 + 0.9 * jax.random.uniform(key_list[6], (TILE_COUNT, TILE_DEPTH_LINES, CAVITY_DEPTH), jnp.float32) ** steps_of(key_list[6], (TILE_COUNT, TILE_DEPTH_LINES, CAVITY_DEPTH), ((0, 128),), -0.2, 0.2), 0.1, 1.0)
    dielectric_line_choice = plant(jax.random.randint(key_list[7], (TILE_COUNT, TILE_DEPTH_LINES, CAVITY_DEPTH), 0, LEVELS), jax.random.fold_in(key_list[7], 1), 0, LEVELS - 1).astype(jnp.int32)
    dielectric_lookup_lines = jnp.clip(jax.random.uniform(key_list[8], (4, LEVELS), jnp.float32, 0.2, 2.0), 0.2, 2.0)
    dispatch_keeper_map = jax.vmap(lambda own: jax.random.permutation(own, DEVICES))(jax.random.split(key_list[9], DEVICES)).reshape((DEVICES, DEVICES)).astype(jnp.int32)
    arrival_position_map = jax.vmap(lambda own: jax.random.permutation(own, DEVICES))(jax.random.split(key_list[10], DEVICES)).reshape((DEVICES, DEVICES)).astype(jnp.int32)
    return dict(efield_vector=efield_vector, hfield_vector=hfield_vector, dielectric_grid=dielectric_grid, sigma_grid=sigma_grid, substance_label=substance_label, thermal_state=thermal_state, wetness_share=wetness_share, dielectric_line_choice=dielectric_line_choice, dielectric_lookup_lines=dielectric_lookup_lines, dispatch_keeper_map=dispatch_keeper_map, arrival_position_map=arrival_position_map)


TIME_STEP = 0.5
DIFFUSION_FACTOR = 0.2
WARMING_FACTOR = 0.5
BOILING = 1.0
EVAP_RATE = 2.0
VAPOUR_ENTHALPY = 0.8


def forward_diff(values, border, along):
    extent = values.shape[along]
    nxt = jnp.concatenate([lax.slice_in_dim(values, 1, extent, axis=along), jnp.expand_dims(border, along)], axis=along)
    return nxt - values


def backward_diff(values, border, along):
    extent = values.shape[along]
    prev = jnp.concatenate([jnp.expand_dims(border, along), lax.slice_in_dim(values, 0, extent - 1, axis=along)], axis=along)
    return values - prev


def zero_border(values, along):
    return jnp.zeros_like(jnp.take(values, 0, axis=along))


def thermal_wetness_advance(thermal_state, wetness_share, deposited_wattage, lookup_factors):
    above_depth_entry = jnp.concatenate([thermal_state[..., 1:], thermal_state[..., -1:]], axis=-1)
    beneath_depth_entry = jnp.concatenate([thermal_state[..., :1], thermal_state[..., :-1]], axis=-1)
    warmed_voxels = thermal_state + DIFFUSION_FACTOR * ((above_depth_entry - thermal_state) + (beneath_depth_entry - thermal_state)) + WARMING_FACTOR * deposited_wattage
    excess = jnp.maximum(warmed_voxels - BOILING, 0.0)
    vaporised_water = wetness_share * (1.0 - jnp.exp(-EVAP_RATE * excess))
    wetness_refreshed = wetness_share - vaporised_water
    warmth_refreshed = warmed_voxels - VAPOUR_ENTHALPY * vaporised_water
    dielectric_refreshed = 1.0 + lookup_factors[0] + 4.0 * lookup_factors[1] * wetness_refreshed
    sigma_refreshed = 0.1 * lookup_factors[2] + 0.3 * lookup_factors[3] * wetness_refreshed
    return warmth_refreshed, wetness_refreshed, dielectric_refreshed, sigma_refreshed


def reference(efield_vector, hfield_vector, dielectric_grid, sigma_grid, substance_label, thermal_state, wetness_share, dielectric_line_choice, dielectric_lookup_lines, dispatch_keeper_map, arrival_position_map):
    elec_x, elec_y, elec_z = efield_vector[0], efield_vector[1], efield_vector[2]
    mag_x, mag_y, mag_z = hfield_vector[0], hfield_vector[1], hfield_vector[2]
    loss_half = sigma_grid * (0.5 * TIME_STEP) / dielectric_grid
    scale_e = (1.0 - loss_half) / (1.0 + loss_half)
    scale_c = (TIME_STEP / dielectric_grid) / (1.0 + loss_half)
    squares = jnp.zeros_like(dielectric_grid)
    for repeat in range(STEPS):
        mag_x = mag_x - TIME_STEP * (forward_diff(elec_z, zero_border(elec_z, 1), 1) - forward_diff(elec_y, zero_border(elec_y, 2), 2))
        mag_y = mag_y - TIME_STEP * (forward_diff(elec_x, zero_border(elec_x, 2), 2) - forward_diff(elec_z, zero_border(elec_z, 0), 0))
        mag_z = mag_z - TIME_STEP * (forward_diff(elec_y, zero_border(elec_y, 0), 0) - forward_diff(elec_x, zero_border(elec_x, 1), 1))
        elec_x = scale_e * elec_x + scale_c * (backward_diff(mag_z, zero_border(mag_z, 1), 1) - backward_diff(mag_y, zero_border(mag_y, 2), 2))
        elec_y = scale_e * elec_y + scale_c * (backward_diff(mag_x, zero_border(mag_x, 2), 2) - backward_diff(mag_z, zero_border(mag_z, 0), 0))
        elec_z = scale_e * elec_z + scale_c * (backward_diff(mag_y, zero_border(mag_y, 0), 0) - backward_diff(mag_x, zero_border(mag_x, 1), 1))
        squares = squares + (elec_x * elec_x + elec_y * elec_y + elec_z * elec_z)
    deposited_wattage = 0.5 * sigma_grid * squares

    devices = N_GX * N_GY
    indices = jnp.arange(devices).astype(jnp.int32)
    inv_send = jnp.argsort(dispatch_keeper_map, axis=1).astype(jnp.int32)
    inv_recv = jnp.argsort(arrival_position_map, axis=1).astype(jnp.int32)

    def to_blocks(values):
        return values.reshape(N_GX, CX, N_GY, CY, CAVITY_DEPTH).transpose(0, 2, 1, 3, 4).reshape(devices, devices, TILE_DEPTH_LINES, CAVITY_DEPTH)

    def from_blocks(blocks):
        return blocks.reshape(N_GX, N_GY, CX, CY, CAVITY_DEPTH).transpose(0, 2, 1, 3, 4).reshape(X, Y, CAVITY_DEPTH)

    blocks = to_blocks(deposited_wattage)
    arrived = blocks[indices[None, :], inv_send.T]
    wattage_each_tile = arrived[indices[:, None], inv_recv].reshape(TILE_COUNT, TILE_DEPTH_LINES, CAVITY_DEPTH)
    lookup_factors = [dielectric_lookup_lines[row][dielectric_line_choice] for row in range(4)]
    warmth_refreshed, wetness_refreshed, dielectric_refreshed, sigma_refreshed = thermal_wetness_advance(thermal_state, wetness_share, wattage_each_tile, lookup_factors)

    def back(values):
        thermal = values.reshape(devices, devices, TILE_DEPTH_LINES, CAVITY_DEPTH)
        slot_rows = thermal[indices[:, None], arrival_position_map]
        return from_blocks(slot_rows[dispatch_keeper_map, indices[:, None]])

    product = substance_label == 2
    dielectric_result = jnp.where(product, back(dielectric_refreshed), dielectric_grid)
    sigma_result = jnp.where(product, back(sigma_refreshed), sigma_grid)
    final_efield = jnp.stack([elec_x, elec_y, elec_z])
    final_hfield = jnp.stack([mag_x, mag_y, mag_z])
    return final_efield, final_hfield, dielectric_result, sigma_result, warmth_refreshed, wetness_refreshed
```

```python
import functools

import jax
import jax.numpy as jnp
from jax import lax
from jax.experimental import pallas as pl
from jax.experimental.pallas import tpu as pltpu
from jax.sharding import PartitionSpec as P

DT = 0.5
MIB = 1 << 20


def passed_along(value, axis, by):
    count = lax.axis_size(axis)
    pairs = [(i, i + by) for i in range(count) if 0 <= i + by < count]
    return lax.ppermute(value, axis, pairs)


def vmem_spec():
    return pl.BlockSpec(memory_space=pltpu.VMEM)


def smem_spec():
    return pl.BlockSpec(memory_space=pltpu.SMEM)


def f32(*shape):
    return jax.ShapeDtypeStruct(shape, jnp.float32)


def dense(count):
    return [vmem_spec()] * count


def limit(mib):
    return pltpu.CompilerParams(vmem_limit_bytes=mib * MIB)


def cost(ops, nbytes):
    return pl.CostEstimate(flops=ops, bytes_accessed=nbytes, transcendentals=0)


def halo_kernel(layer_ref, e_ref, sx_ref, sy_ref):
    sx_ref[0] = layer_ref[1, 0]
    sx_ref[1] = layer_ref[2, 0]
    for x in range(e_ref.shape[1]):
        sy_ref[0, x : x + 1, :] = e_ref[0, x, 0:1, :]
        sy_ref[1, x : x + 1, :] = e_ref[2, x, 0:1, :]


def first_halo(efield):
    _, nx, ny, nz = efield.shape
    return pl.pallas_call(
        halo_kernel,
        grid=(1,),
        in_specs=[
            pl.BlockSpec((3, 1, ny, nz), lambda i: (0, 0, 0, 0)),
            pl.BlockSpec((3, nx, 8, nz), lambda i: (0, 0, 0, 0)),
        ],
        out_specs=[vmem_spec(), vmem_spec()],
        out_shape=[f32(2, ny, nz), f32(2, nx, nz)],
        compiler_params=limit(4),
        name="halo",
    )(efield, efield)


def patch_last(value, row):
    ny, nz = value.shape
    at = lax.broadcasted_iota(jnp.int32, (8, nz), 0) == 7
    return jnp.concatenate([value[: ny - 8], jnp.where(at, row, value[ny - 8 :])], axis=0)


def patch_first(value, row):
    nz = value.shape[1]
    at = lax.broadcasted_iota(jnp.int32, (8, nz), 0) == 0
    return jnp.concatenate([jnp.where(at, row, value[:8]), value[8:]], axis=0)


def fwd_z(f):
    ny, nz = f.shape
    lane = lax.broadcasted_iota(jnp.int32, f.shape, 1)
    return jnp.where(lane == nz - 1, 0.0, pltpu.roll(f, nz - 1, 1)) - f


def bwd_z(f):
    lane = lax.broadcasted_iota(jnp.int32, f.shape, 1)
    return f - jnp.where(lane == 0, 0.0, pltpu.roll(f, 1, 1))


def fwd_y(f):
    ny = f.shape[0]
    return patch_last(pltpu.roll(f, ny - 1, 0), 0.0) - f


def bwd_y(f):
    return f - patch_first(pltpu.roll(f, 1, 0), 0.0)


def e_slab(x, first, e_ref, layer_ref, rows_ref):
    ex, ey, ez = e_ref[0, x], e_ref[1, x], e_ref[2, x]
    if rows_ref is not None:
        ex = patch_first(ex, rows_ref[0, pl.ds(x, 1), :])
        if first:
            ey, ez = layer_ref[0], layer_ref[1]
        else:
            ez = patch_first(ez, rows_ref[1, pl.ds(x, 1), :])
    return ex, ey, ez


def h_slab(x, last, h_ref, layer_ref, rows_ref):
    hx, hy, hz = h_ref[0, x], h_ref[1, x], h_ref[2, x]
    if rows_ref is not None:
        hx = patch_last(hx, rows_ref[0, pl.ds(x, 1), :])
        if last:
            hy, hz = layer_ref[0], layer_ref[1]
        else:
            hz = patch_last(hz, rows_ref[1, pl.ds(x, 1), :])
    return hx, hy, hz


def h_kernel(fixed, *refs):
    if fixed:
        e_ref, el_ref, er_ref, h_ref, hl_ref, hr_ref, out_ref, layer_ref, rows_ref = refs
    else:
        e_ref, h_ref, out_ref, layer_ref, rows_ref = refs
        el_ref = er_ref = hl_ref = hr_ref = None
    nx, ny, nz = e_ref.shape[1:]

    def slab(x, first, last):
        ex, ey, ez = e_slab(x, first, e_ref, el_ref, er_ref)
        hx, hy, hz = h_slab(x, last, h_ref, hl_ref, hr_ref)
        if last:
            ey_step, ez_step = -ey, -ez
        else:
            _, ey_next, ez_next = e_slab(x + 1, False, e_ref, el_ref, er_ref)
            ey_step, ez_step = ey_next - ey, ez_next - ez
        hx = hx - DT * (fwd_y(ez) - fwd_z(ey))
        hy = hy - DT * (fwd_z(ex) - ez_step)
        hz = hz - DT * (ey_step - fwd_y(ex))
        out_ref[0, x] = hx
        out_ref[1, x] = hy
        out_ref[2, x] = hz
        rows_ref[0, pl.ds(x, 1), :] = hx[ny - 1 : ny]
        rows_ref[1, pl.ds(x, 1), :] = hz[ny - 1 : ny]
        if last:
            layer_ref[0] = hy
            layer_ref[1] = hz

    slab(0, True, False)
    lax.fori_loop(1, nx - 1, lambda x, c: (slab(x, False, False), c)[1], 0)
    slab(nx - 1, False, True)


def h_update(efield, e_fix, hfield, h_fix):
    _, nx, ny, nz = efield.shape
    args = [efield, *e_fix, hfield, *h_fix]
    return pl.pallas_call(
        functools.partial(h_kernel, bool(e_fix)),
        in_specs=dense(len(args)),
        out_specs=dense(3),
        out_shape=[f32(3, nx, ny, nz), f32(2, ny, nz), f32(2, nx, nz)],
        compiler_params=limit(16),
        cost_estimate=cost(40 * nx * ny * nz, 9 * MIB),
        name="hstep",
    )(*args)


def h_border_kernel(layer_ref, rows_ref, gx_ref, gy_ref, layer_out, rows_out):
    ny, nx = layer_ref.shape[1], rows_ref.shape[1]
    layer_out[0] = layer_ref[0] + DT * gx_ref[1]
    layer_out[1] = patch_last(
        layer_ref[1] - DT * gx_ref[0],
        layer_ref[1, ny - 1 : ny] - DT * gx_ref[0, ny - 1 : ny] + DT * gy_ref[0, nx - 1 : nx],
    )
    rows_out[0] = rows_ref[0] - DT * gy_ref[1]
    rows_out[1] = patch_last(
        rows_ref[1] + DT * gy_ref[0],
        rows_ref[1, nx - 1 : nx] - DT * gx_ref[0, ny - 1 : ny] + DT * gy_ref[0, nx - 1 : nx],
    )


def h_border(layer, rows, gx, gy):
    return pl.pallas_call(
        h_border_kernel,
        in_specs=dense(4),
        out_specs=dense(2),
        out_shape=[f32(*layer.shape), f32(*rows.shape)],
        compiler_params=limit(2),
        name="hborder",
    )(layer, rows, gx, gy)


def e_kernel(fixed, final, *refs):
    refs = list(refs)
    e_ref = refs.pop(0)
    el_ref, er_ref = (refs.pop(0), refs.pop(0)) if fixed else (None, None)
    h_ref, hl_ref, hr_ref, eps_ref, sig_ref, out_ref, layer_ref, rows_ref = refs[:8]
    nx, ny, nz = e_ref.shape[1:]

    def slab(x, first, last):
        hx, hy, hz = h_slab(x, last, h_ref, hl_ref, hr_ref)
        if first:
            hy_step, hz_step = hy, hz
        else:
            _, hy_prev, hz_prev = h_slab(x - 1, False, h_ref, hl_ref, hr_ref)
            hy_step, hz_step = hy - hy_prev, hz - hz_prev
        sig = sig_ref[x]
        quarter = 0.25 * sig
        eps = eps_ref[x]
        inv = 1.0 / (eps + quarter)
        scale_e = (eps - quarter) * inv
        scale_c = DT * inv
        ex0, ey0, ez0 = e_slab(x, first, e_ref, el_ref, er_ref)
        ex = scale_e * ex0 + scale_c * (bwd_y(hz) - bwd_z(hy))
        ey = scale_e * ey0 + scale_c * (bwd_z(hx) - hz_step)
        ez = scale_e * ez0 + scale_c * (hy_step - bwd_y(hx))
        out_ref[0, x] = ex
        out_ref[1, x] = ey
        out_ref[2, x] = ez
        at = pl.ds(x, 1)
        rows_ref[0, at, :] = ex[0:1]
        rows_ref[1, at, :] = ez[0:1]
        rows_ref[2, at, :] = scale_c[0:1]
        if first:
            layer_ref[0] = ey
            layer_ref[1] = ez
            layer_ref[2] = scale_c
        if final:
            before = ex0 * ex0 + ey0 * ey0 + ez0 * ez0
            half = 0.5 * sig
            refs[8][x] = half * (before + (ex * ex + ey * ey + ez * ez))
            rows_ref[3, at, :] = ey[0:1]
            rows_ref[4, at, :] = before[0:1]
            rows_ref[5, at, :] = half[0:1]
            if first:
                layer_ref[3] = ex
                layer_ref[4] = before
                layer_ref[5] = half

    slab(0, True, False)
    lax.fori_loop(1, nx - 1, lambda x, c: (slab(x, False, False), c)[1], 0)
    slab(nx - 1, False, True)


def e_update(efield, e_fix, hfield, h_fix, eps, sig, final):
    _, nx, ny, nz = efield.shape
    args = [efield, *e_fix, hfield, *h_fix, eps, sig]
    kept = 6 if final else 3
    outs = [f32(3, nx, ny, nz), f32(kept, ny, nz), f32(kept, nx, nz)]
    if final:
        outs.append(f32(nx, ny, nz))
    return pl.pallas_call(
        functools.partial(e_kernel, bool(e_fix), final),
        in_specs=dense(len(args)),
        out_specs=dense(len(outs)),
        out_shape=outs,
        compiler_params=limit(20),
        cost_estimate=cost(60 * nx * ny * nz, 11 * MIB),
        name="estep",
    )(*args)


def e_border_values(layer_ref, rows_ref, gx_ref, gy_ref):
    ey_layer = layer_ref[0] + layer_ref[2] * gx_ref[1]
    ez_layer = layer_ref[1] - layer_ref[2] * gx_ref[0]
    ez_layer = patch_first(ez_layer, ez_layer[0:1] + layer_ref[2, 0:1] * gy_ref[0, 0:1])
    ex_rows = rows_ref[0] - rows_ref[2] * gy_ref[1]
    ez_rows = patch_first(rows_ref[1] + rows_ref[2] * gy_ref[0], ez_layer[0:1])
    return ey_layer, ez_layer, ex_rows, ez_rows


def e_border_kernel(layer_ref, rows_ref, gx_ref, gy_ref, layer_out, rows_out):
    layer_out[0], layer_out[1], rows_out[0], rows_out[1] = e_border_values(
        layer_ref, rows_ref, gx_ref, gy_ref
    )


def e_border(layer, rows, gx, gy):
    return pl.pallas_call(
        e_border_kernel,
        in_specs=dense(4),
        out_specs=dense(2),
        out_shape=[f32(*gx.shape), f32(*gy.shape)],
        compiler_params=limit(2),
        name="eborder",
    )(layer, rows, gx, gy)


def power_kernel(dest, p_ref, layer_ref, rows_ref, gx_ref, gy_ref, out_ref, layer_out, rows_out, scratch):
    nx, ny, nz = p_ref.shape
    parts = ny // 8
    ey_layer, ez_layer, ex_rows, ez_rows = e_border_values(layer_ref, rows_ref, gx_ref, gy_ref)
    layer_out[0], layer_out[1], rows_out[0], rows_out[1] = ey_layer, ez_layer, ex_rows, ez_rows
    ex_layer = patch_first(layer_ref[3], ex_rows[0:1])
    squares = ex_layer * ex_layer + ey_layer * ey_layer + ez_layer * ez_layer
    layer_power = layer_ref[5] * (layer_ref[4] + squares)
    ey_rows = rows_ref[3]
    squares = ex_rows * ex_rows + ey_rows * ey_rows + ez_rows * ez_rows
    scratch[...] = rows_ref[5] * (rows_ref[4] + squares)
    top = lax.broadcasted_iota(jnp.int32, (8, nz), 0) == 0

    for part in range(parts):
        out_ref[dest[0, part]] = layer_power[part * 8 : part * 8 + 8]

    def body(x, carry):
        row = scratch[pl.ds(x, 1), :]
        out_ref[dest[0, x * parts]] = jnp.where(top, row, p_ref[x, 0:8, :])
        for part in range(1, parts):
            out_ref[dest[0, x * parts + part]] = p_ref[x, part * 8 : part * 8 + 8, :]
        return carry

    lax.fori_loop(1, nx, body, 0, unroll=2)


def power_border(dest, power, layer, rows, gx, gy):
    nx, ny, nz = power.shape
    return pl.pallas_call(
        power_kernel,
        in_specs=[smem_spec()] + dense(5),
        out_specs=dense(3),
        out_shape=[f32(nx * ny // 8, 8, nz), f32(*gx.shape), f32(*gy.shape)],
        scratch_shapes=[pltpu.VMEM((nx, nz), jnp.float32)],
        compiler_params=limit(8),
        cost_estimate=cost(4 * nx * ny * nz, 2 * MIB),
        name="power",
    )(dest, power, layer, rows, gx, gy)


def flush_kernel(e_ref, el_ref, er_ref, h_ref, hl_ref, hr_ref, e_out, h_out):
    nx = e_ref.shape[1]

    def slab(x, first, last):
        e_out[0, x], e_out[1, x], e_out[2, x] = e_slab(x, first, e_ref, el_ref, er_ref)
        h_out[0, x], h_out[1, x], h_out[2, x] = h_slab(x, last, h_ref, hl_ref, hr_ref)

    slab(0, True, False)
    lax.fori_loop(1, nx - 1, lambda x, c: (slab(x, False, False), c)[1], 0)
    slab(nx - 1, False, True)


def flush(efield, e_fix, hfield, h_fix):
    return pl.pallas_call(
        flush_kernel,
        in_specs=dense(6),
        out_specs=dense(2),
        out_shape=[f32(*efield.shape), f32(*hfield.shape)],
        compiler_params=limit(16),
        cost_estimate=cost(efield.size, 12 * MIB),
        name="flush",
    )(efield, *e_fix, hfield, *h_fix)


def lookup_kernel(lines, choice_ref, out_ref):
    levels = lines.shape[1]

    def body(j, carry):
        choice = choice_ref[j]
        factors = [jnp.full(choice.shape, lines[c, 0], jnp.float32) for c in range(4)]
        for level in range(1, levels):
            match = choice == level
            for c in range(4):
                factors[c] = jnp.where(match, lines[c, level], factors[c])
        out_ref[0, j] = 1.0 + factors[0]
        out_ref[1, j] = 4.0 * factors[1]
        out_ref[2, j] = 0.1 * factors[2]
        out_ref[3, j] = 0.3 * factors[3]
        return carry

    lax.fori_loop(0, choice_ref.shape[0], body, 0, unroll=2)


def lookup(lines, choice):
    n, width, nz = choice.shape
    return pl.pallas_call(
        lookup_kernel,
        in_specs=[smem_spec(), vmem_spec()],
        out_specs=vmem_spec(),
        out_shape=f32(4, n, width, nz),
        compiler_params=limit(10),
        cost_estimate=cost(80 * n * width * nz, 5 * MIB),
        name="lookup",
    )(lines, choice)


def thermal_kernel(arrive, p_ref, t_ref, w_ref, f_ref, send_out, t_out, w_out):
    n, width, nz = p_ref.shape
    lane = lax.broadcasted_iota(jnp.int32, (width, nz), 1)

    def body(s, carry):
        slot = arrive[0, s]
        state = t_ref[slot]
        above = jnp.where(lane == nz - 1, state, pltpu.roll(state, nz - 1, 1))
        below = jnp.where(lane == 0, state, pltpu.roll(state, 1, 1))
        heated = state + 0.2 * ((above - state) + (below - state)) + 0.5 * p_ref[s]
        wet = w_ref[slot]
        gone = wet * (1.0 - jnp.exp(-2.0 * jnp.maximum(heated - 1.0, 0.0)))
        left = wet - gone
        w_out[slot] = left
        t_out[slot] = heated - 0.8 * gone
        send_out[s, 0:width, :] = f_ref[0, slot] + f_ref[1, slot] * left
        send_out[s, width : 2 * width, :] = f_ref[2, slot] + f_ref[3, slot] * left
        return carry

    lax.fori_loop(0, n, body, 0, unroll=4)


def thermal(arrive, power, state, wetness, factors):
    n, width, nz = power.shape
    return pl.pallas_call(
        thermal_kernel,
        in_specs=[smem_spec()] + dense(4),
        out_specs=dense(3),
        out_shape=[f32(n, 2 * width, nz), f32(n, width, nz), f32(n, width, nz)],
        compiler_params=limit(20),
        cost_estimate=cost(40 * n * width * nz, 11 * MIB),
        name="thermal",
    )(arrive, power, state, wetness, factors)


def select_kernel(dest, recv_ref, eps_ref, sig_ref, lab_ref, eps_out, sig_out):
    nx, ny, nz = eps_out.shape
    parts = ny // 8

    def body(x, carry):
        for part in range(parts):
            row = dest[0, x * parts + part]
            rows = slice(part * 8, part * 8 + 8)
            product = lab_ref[x, rows, :] == 2
            eps_out[x, rows, :] = jnp.where(product, recv_ref[row, 0:8, :], eps_ref[x, rows, :])
            sig_out[x, rows, :] = jnp.where(product, recv_ref[row, 8:16, :], sig_ref[x, rows, :])
        return carry

    lax.fori_loop(0, nx, body, 0, unroll=2)


def select(dest, recv, eps, sig, label):
    nx, ny, nz = eps.shape
    return pl.pallas_call(
        select_kernel,
        in_specs=[smem_spec()] + dense(4),
        out_specs=dense(2),
        out_shape=[f32(nx, ny, nz), f32(nx, ny, nz)],
        compiler_params=limit(12),
        cost_estimate=cost(4 * nx * ny * nz, 7 * MIB),
        name="select",
    )(dest, recv, eps, sig, label)


def exchange(value):
    return lax.all_to_all(value, ("gx", "gy"), split_axis=0, concat_axis=0, tiled=True)


def borders(layer, rows, by):
    return passed_along(layer, "gx", by), passed_along(rows, "gy", by)


def local(
    efield_vector,
    hfield_vector,
    dielectric_grid,
    sigma_grid,
    substance_label,
    thermal_state,
    wetness_share,
    dielectric_line_choice,
    dielectric_lookup_lines,
    dispatch_keeper_map,
    arrival_position_map,
):
    efield, hfield = efield_vector, hfield_vector
    e_fix, h_fix = (), ()
    layer, rows = first_halo(efield)
    for step in range(2):
        gx, gy = borders(layer, rows, -1)
        hfield, layer, rows = h_update(efield, e_fix, hfield, h_fix)
        h_fix = h_border(layer, rows, gx, gy)
        gx, gy = borders(*h_fix, 1)
        final = step == 1
        efield, layer, rows, *power = e_update(
            efield, e_fix, hfield, h_fix, dielectric_grid, sigma_grid, final
        )
        if final:
            power, *e_fix = power_border(dispatch_keeper_map, power[0], layer, rows, gx, gy)
        else:
            e_fix = layer, rows = e_border(layer, rows, gx, gy)
    arrived = exchange(power)
    factors = lookup(dielectric_lookup_lines, dielectric_line_choice)
    final_efield, final_hfield = flush(efield, e_fix, hfield, h_fix)
    outgoing, warmth, moisture = thermal(
        arrival_position_map, arrived, thermal_state, wetness_share, factors
    )
    returned = exchange(outgoing)
    dielectric_result, sigma_result = select(
        dispatch_keeper_map, returned, dielectric_grid, sigma_grid, substance_label
    )
    return final_efield, final_hfield, dielectric_result, sigma_result, warmth, moisture


def solution(mesh):
    in_specs = (
        P(None, "gx", "gy", None),
        P(None, "gx", "gy", None),
        P("gx", "gy", None),
        P("gx", "gy", None),
        P("gx", "gy", None),
        P(("gx", "gy"), None, None),
        P(("gx", "gy"), None, None),
        P(("gx", "gy"), None, None),
        P(),
        P(("gx", "gy"), None),
        P(("gx", "gy"), None),
    )
    out_specs = (
        P(None, "gx", "gy", None),
        P(None, "gx", "gy", None),
        P("gx", "gy", None),
        P("gx", "gy", None),
        P(("gx", "gy"), None, None),
        P(("gx", "gy"), None, None),
    )
    return jax.shard_map(local, mesh=mesh, in_specs=in_specs, out_specs=out_specs, check_vma=False)
```

```python
import functools

import jax
import jax.numpy as jnp
from jax import lax
from jax.experimental import pallas as pl
from jax.experimental.pallas import tpu as pltpu
from jax.sharding import PartitionSpec as P

DT = 0.5
MIB = 1 << 20
GROUP = 10
FAR = 5
THERMAL_MIB = 62


def passed_along(value, axis, by):
    count = lax.axis_size(axis)
    pairs = [(i, i + by) for i in range(count) if 0 <= i + by < count]
    return lax.ppermute(value, axis, pairs)


def vmem_spec():
    return pl.BlockSpec(memory_space=pltpu.VMEM)


def smem_spec():
    return pl.BlockSpec(memory_space=pltpu.SMEM)


def f32(*shape):
    return jax.ShapeDtypeStruct(shape, jnp.float32)


def dense(count):
    return [vmem_spec()] * count


def limit(mib):
    return pltpu.CompilerParams(vmem_limit_bytes=mib * MIB)


def hbm_spec():
    return pl.BlockSpec(memory_space=pltpu.HBM)


def part_of(ref, axis, chunk, chunks):
    size = ref.shape[axis] // chunks
    where = [slice(None)] * axis + [pl.ds(chunk * size, size)]
    return ref.at[tuple(where)]


def copies(sources, targets, sem, chunks, axis=0):
    return [
        [
            pltpu.make_async_copy(
                part_of(source, axis, chunk, chunks), part_of(target, axis, chunk, chunks), sem.at[k, chunk]
            )
            for k, (source, target) in enumerate(zip(sources, targets))
        ]
        for chunk in range(chunks)
    ]


def hbm(*shape):
    return pltpu.HBM(shape, jnp.float32)


def cost(ops, nbytes):
    return pl.CostEstimate(flops=ops, bytes_accessed=nbytes, transcendentals=0)


def halo_kernel(layer_ref, e_ref, sx_ref, sy_ref):
    sx_ref[0] = layer_ref[1, 0]
    sx_ref[1] = layer_ref[2, 0]
    for x in range(e_ref.shape[1]):
        sy_ref[0, x : x + 1, :] = e_ref[0, x, 0:1, :]
        sy_ref[1, x : x + 1, :] = e_ref[2, x, 0:1, :]


def first_halo(efield):
    _, nx, ny, nz = efield.shape
    return pl.pallas_call(
        halo_kernel,
        grid=(1,),
        in_specs=[
            pl.BlockSpec((3, 1, ny, nz), lambda i: (0, 0, 0, 0)),
            pl.BlockSpec((3, nx, 8, nz), lambda i: (0, 0, 0, 0)),
        ],
        out_specs=[vmem_spec(), vmem_spec()],
        out_shape=[f32(2, ny, nz), f32(2, nx, nz)],
        compiler_params=limit(4),
        name="halo",
    )(efield, efield)


def patch_last(value, row):
    ny, nz = value.shape
    at = lax.broadcasted_iota(jnp.int32, (8, nz), 0) == 7
    return jnp.concatenate([value[: ny - 8], jnp.where(at, row, value[ny - 8 :])], axis=0)


def patch_first(value, row):
    nz = value.shape[1]
    at = lax.broadcasted_iota(jnp.int32, (8, nz), 0) == 0
    return jnp.concatenate([jnp.where(at, row, value[:8]), value[8:]], axis=0)


def fwd_z(f):
    ny, nz = f.shape
    lane = lax.broadcasted_iota(jnp.int32, f.shape, 1)
    return jnp.where(lane == nz - 1, 0.0, pltpu.roll(f, nz - 1, 1)) - f


def bwd_z(f):
    lane = lax.broadcasted_iota(jnp.int32, f.shape, 1)
    return f - jnp.where(lane == 0, 0.0, pltpu.roll(f, 1, 1))


def fwd_y(f):
    ny = f.shape[0]
    return patch_last(pltpu.roll(f, ny - 1, 0), 0.0) - f


def bwd_y(f):
    return f - patch_first(pltpu.roll(f, 1, 0), 0.0)


def e_slab(x, first, e_ref, layer_ref, rows_ref):
    ex, ey, ez = e_ref[0, x], e_ref[1, x], e_ref[2, x]
    if rows_ref is not None:
        ex = patch_first(ex, rows_ref[0, pl.ds(x, 1), :])
        if first:
            ey, ez = layer_ref[0], layer_ref[1]
        else:
            ez = patch_first(ez, rows_ref[1, pl.ds(x, 1), :])
    return ex, ey, ez


def h_slab(x, last, h_ref, layer_ref, rows_ref):
    hx, hy, hz = h_ref[0, x], h_ref[1, x], h_ref[2, x]
    if rows_ref is not None:
        hx = patch_last(hx, rows_ref[0, pl.ds(x, 1), :])
        if last:
            hy, hz = layer_ref[0], layer_ref[1]
        else:
            hz = patch_last(hz, rows_ref[1, pl.ds(x, 1), :])
    return hx, hy, hz


def parts_of_copy(source, target, sem):
    return [pltpu.make_async_copy(source.at[k], target.at[k], sem.at[k]) for k in range(source.shape[0])]


def walk(slab, nx):
    groups = (nx - 2) // GROUP
    slab(0, True, False)

    def body(g, carry):
        for k in range(GROUP):
            slab(1 + g * GROUP + k, False, False)
        return carry

    lax.fori_loop(0, groups, body, 0)
    for x in range(1 + groups * GROUP, nx - 1):
        slab(x, False, False)
    slab(nx - 1, False, True)


def h_kernel(fixed, *refs):
    if fixed:
        e_ref, el_ref, er_ref, h_ref, hl_ref, hr_ref, out_ref, layer_ref, rows_ref, out_hbm, sem = refs
    else:
        e_ref, h_ref, out_ref, layer_ref, rows_ref = refs
        el_ref = er_ref = hl_ref = hr_ref = None
    nx, ny, nz = e_ref.shape[1:]

    def slab(x, first, last):
        ex, ey, ez = e_slab(x, first, e_ref, el_ref, er_ref)
        hx, hy, hz = h_slab(x, last, h_ref, hl_ref, hr_ref)
        if last:
            ey_step, ez_step = -ey, -ez
        else:
            _, ey_next, ez_next = e_slab(x + 1, False, e_ref, el_ref, er_ref)
            ey_step, ez_step = ey_next - ey, ez_next - ez
        hx = hx - DT * (fwd_y(ez) - fwd_z(ey))
        hy = hy - DT * (fwd_z(ex) - ez_step)
        hz = hz - DT * (ey_step - fwd_y(ex))
        out_ref[0, x] = hx
        out_ref[1, x] = hy
        out_ref[2, x] = hz
        rows_ref[0, pl.ds(x, 1), :] = hx[ny - 1 : ny]
        rows_ref[1, pl.ds(x, 1), :] = hz[ny - 1 : ny]
        if last:
            layer_ref[0] = hy
            layer_ref[1] = hz

    walk(slab, nx)
    if fixed:
        moves = parts_of_copy(out_ref, out_hbm, sem)
        for move in moves:
            move.start()
        for move in moves:
            move.wait()


def h_update(efield, e_fix, hfield, h_fix):
    _, nx, ny, nz = efield.shape
    args = [efield, *e_fix, hfield, *h_fix]
    outs = [f32(3, nx, ny, nz), f32(2, ny, nz), f32(2, nx, nz)]
    return pl.pallas_call(
        functools.partial(h_kernel, bool(e_fix)),
        in_specs=dense(len(args)),
        out_specs=dense(3) + [hbm_spec()] * bool(e_fix),
        out_shape=outs + [hbm(3, nx, ny, nz)] * bool(e_fix),
        scratch_shapes=[pltpu.SemaphoreType.DMA((3,))] * bool(e_fix),
        compiler_params=limit(16),
        cost_estimate=cost(40 * nx * ny * nz, 9 * MIB),
        name="hstep",
    )(*args)


def h_border_kernel(layer_ref, rows_ref, gx_ref, gy_ref, layer_out, rows_out):
    ny, nx = layer_ref.shape[1], rows_ref.shape[1]
    layer_out[0] = layer_ref[0] + DT * gx_ref[1]
    layer_out[1] = patch_last(
        layer_ref[1] - DT * gx_ref[0],
        layer_ref[1, ny - 1 : ny] - DT * gx_ref[0, ny - 1 : ny] + DT * gy_ref[0, nx - 1 : nx],
    )
    rows_out[0] = rows_ref[0] - DT * gy_ref[1]
    rows_out[1] = patch_last(
        rows_ref[1] + DT * gy_ref[0],
        rows_ref[1, nx - 1 : nx] - DT * gx_ref[0, ny - 1 : ny] + DT * gy_ref[0, nx - 1 : nx],
    )


def h_border(layer, rows, gx, gy):
    return pl.pallas_call(
        h_border_kernel,
        in_specs=dense(4),
        out_specs=dense(2),
        out_shape=[f32(*layer.shape), f32(*rows.shape)],
        compiler_params=limit(2),
        name="hborder",
    )(layer, rows, gx, gy)


def e_kernel(fixed, final, *refs):
    refs = list(refs)
    e_ref = refs.pop(0)
    el_ref, er_ref = (refs.pop(0), refs.pop(0)) if fixed else (None, None)
    h_ref, hl_ref, hr_ref, eps_ref, sig_ref, out_ref, layer_ref, rows_ref = refs[:8]
    nx, ny, nz = e_ref.shape[1:]

    def slab(x, first, last):
        hx, hy, hz = h_slab(x, last, h_ref, hl_ref, hr_ref)
        if first:
            hy_step, hz_step = hy, hz
        else:
            _, hy_prev, hz_prev = h_slab(x - 1, False, h_ref, hl_ref, hr_ref)
            hy_step, hz_step = hy - hy_prev, hz - hz_prev
        sig = sig_ref[x]
        quarter = 0.25 * sig
        eps = eps_ref[x]
        inv = 1.0 / (eps + quarter)
        scale_e = (eps - quarter) * inv
        scale_c = DT * inv
        ex0, ey0, ez0 = e_slab(x, first, e_ref, el_ref, er_ref)
        ex = scale_e * ex0 + scale_c * (bwd_y(hz) - bwd_z(hy))
        ey = scale_e * ey0 + scale_c * (bwd_z(hx) - hz_step)
        ez = scale_e * ez0 + scale_c * (hy_step - bwd_y(hx))
        out_ref[0, x] = ex
        out_ref[1, x] = ey
        out_ref[2, x] = ez
        at = pl.ds(x, 1)
        rows_ref[0, at, :] = ex[0:1]
        rows_ref[1, at, :] = ez[0:1]
        rows_ref[2, at, :] = scale_c[0:1]
        if first:
            layer_ref[0] = ey
            layer_ref[1] = ez
            layer_ref[2] = scale_c
        if final:
            before = ex0 * ex0 + ey0 * ey0 + ez0 * ez0
            half = 0.5 * sig
            refs[8][x] = half * (before + (ex * ex + ey * ey + ez * ez))
            rows_ref[3, at, :] = ey[0:1]
            rows_ref[4, at, :] = before[0:1]
            rows_ref[5, at, :] = half[0:1]
            if first:
                layer_ref[3] = ex
                layer_ref[4] = before
                layer_ref[5] = half

    walk(slab, nx)


def e_update(efield, e_fix, hfield, h_fix, eps, sig, final):
    _, nx, ny, nz = efield.shape
    args = [efield, *e_fix, hfield, *h_fix, eps, sig]
    kept = 6 if final else 3
    outs = [f32(3, nx, ny, nz), f32(kept, ny, nz), f32(kept, nx, nz)]
    if final:
        outs.append(f32(nx, ny, nz))
    return pl.pallas_call(
        functools.partial(e_kernel, bool(e_fix), final),
        in_specs=dense(len(args)),
        out_specs=dense(len(outs)),
        out_shape=outs,
        compiler_params=limit(16),
        cost_estimate=cost(60 * nx * ny * nz, 11 * MIB),
        name="estep",
    )(*args)


def e_border_values(layer_ref, rows_ref, gx_ref, gy_ref):
    ey_layer = layer_ref[0] + layer_ref[2] * gx_ref[1]
    ez_layer = layer_ref[1] - layer_ref[2] * gx_ref[0]
    ez_layer = patch_first(ez_layer, ez_layer[0:1] + layer_ref[2, 0:1] * gy_ref[0, 0:1])
    ex_rows = rows_ref[0] - rows_ref[2] * gy_ref[1]
    ez_rows = patch_first(rows_ref[1] + rows_ref[2] * gy_ref[0], ez_layer[0:1])
    return ey_layer, ez_layer, ex_rows, ez_rows


def e_border_kernel(layer_ref, rows_ref, gx_ref, gy_ref, layer_out, rows_out):
    layer_out[0], layer_out[1], rows_out[0], rows_out[1] = e_border_values(
        layer_ref, rows_ref, gx_ref, gy_ref
    )


def e_border(layer, rows, gx, gy):
    return pl.pallas_call(
        e_border_kernel,
        in_specs=dense(4),
        out_specs=dense(2),
        out_shape=[f32(*gx.shape), f32(*gy.shape)],
        compiler_params=limit(2),
        name="eborder",
    )(layer, rows, gx, gy)


def power_kernel(dest, e_ref, p_ref, layer_ref, rows_ref, gx_ref, gy_ref, out_hbm, layer_out, rows_out, e_hbm, scratch, out_ref, sem, e_sem):
    moves = parts_of_copy(e_ref, e_hbm, e_sem)
    for move in moves:
        move.start()
    nx, ny, nz = p_ref.shape
    parts = ny // 8
    ey_layer, ez_layer, ex_rows, ez_rows = e_border_values(layer_ref, rows_ref, gx_ref, gy_ref)
    layer_out[0], layer_out[1], rows_out[0], rows_out[1] = ey_layer, ez_layer, ex_rows, ez_rows
    ex_layer = patch_first(layer_ref[3], ex_rows[0:1])
    squares = ex_layer * ex_layer + ey_layer * ey_layer + ez_layer * ez_layer
    layer_power = layer_ref[5] * (layer_ref[4] + squares)
    ey_rows = rows_ref[3]
    squares = ex_rows * ex_rows + ey_rows * ey_rows + ez_rows * ez_rows
    scratch[...] = rows_ref[5] * (rows_ref[4] + squares)
    top = lax.broadcasted_iota(jnp.int32, (8, nz), 0) == 0

    for part in range(parts):
        out_ref[dest[0, part]] = layer_power[part * 8 : part * 8 + 8]

    def body(x, carry):
        row = scratch[pl.ds(x, 1), :]
        out_ref[dest[0, x * parts]] = jnp.where(top, row, p_ref[x, 0:8, :])
        for part in range(1, parts):
            out_ref[dest[0, x * parts + part]] = p_ref[x, part * 8 : part * 8 + 8, :]
        return carry

    lax.fori_loop(1, nx, body, 0, unroll=2)
    moves.append(pltpu.make_async_copy(out_ref, out_hbm, sem))
    moves[-1].start()
    for move in moves:
        move.wait()


def power_border(dest, efield, power, layer, rows, gx, gy):
    nx, ny, nz = power.shape
    return pl.pallas_call(
        power_kernel,
        in_specs=[smem_spec()] + dense(6),
        out_specs=[hbm_spec()] + dense(2) + [hbm_spec()],
        out_shape=[hbm(nx * ny // 8, 8, nz), f32(*gx.shape), f32(*gy.shape), hbm(*efield.shape)],
        scratch_shapes=[
            pltpu.VMEM((nx, nz), jnp.float32),
            pltpu.VMEM((nx * ny // 8, 8, nz), jnp.float32),
            pltpu.SemaphoreType.DMA(()),
            pltpu.SemaphoreType.DMA((3,)),
        ],
        compiler_params=limit(8),
        cost_estimate=cost(4 * nx * ny * nz, 8 * MIB),
        name="power",
    )(dest, efield, power, layer, rows, gx, gy)


def flush_kernel(e_ref, el_ref, er_ref, h_ref, hl_ref, hr_ref, e_out, h_out):
    nx = e_ref.shape[1]

    def slab(x, first, last):
        e_out[0, x], e_out[1, x], e_out[2, x] = e_slab(x, first, e_ref, el_ref, er_ref)
        h_out[0, x], h_out[1, x], h_out[2, x] = h_slab(x, last, h_ref, hl_ref, hr_ref)

    slab(0, True, False)
    lax.fori_loop(1, nx - 1, lambda x, c: (slab(x, False, False), c)[1], 0)
    slab(nx - 1, False, True)


def flush(efield, e_fix, hfield, h_fix):
    return pl.pallas_call(
        flush_kernel,
        in_specs=dense(6),
        out_specs=dense(2),
        out_shape=[f32(*efield.shape), f32(*hfield.shape)],
        compiler_params=limit(16),
        cost_estimate=cost(efield.size, 12 * MIB),
        name="flush",
    )(efield, *e_fix, hfield, *h_fix)


def pack_kernel(arrive, lines, t_ref, w_ref, c_ref, *out_refs):
    rows = out_refs[0].shape[0]
    width, nz = t_ref.shape[1:]
    levels = lines.shape[1]
    step = pl.program_id(0)
    lane = lax.broadcasted_iota(jnp.int32, (width, nz), 1)

    def body(r, carry):
        slot = arrive[0, step * rows + r]
        state = t_ref[slot]
        choice = c_ref[slot]
        above = jnp.where(lane == nz - 1, state, pltpu.roll(state, nz - 1, 1))
        below = jnp.where(lane == 0, state, pltpu.roll(state, 1, 1))
        factors = [jnp.full(choice.shape, lines[c, 0], jnp.float32) for c in range(4)]
        for level in range(1, levels):
            match = choice == level
            for c in range(4):
                factors[c] = jnp.where(match, lines[c, level], factors[c])
        wet = w_ref[slot]
        values = [
            state + 0.2 * ((above - state) + (below - state)),
            1.0 + factors[0],
            4.0 * factors[1] * wet,
            0.1 * factors[2],
            0.3 * factors[3] * wet,
        ]
        for k, value in enumerate(values):
            target, at = (out_refs[0], k) if k < FAR else (out_refs[1], k - FAR)
            target[r, at * width : (at + 1) * width, :] = value
        return carry

    lax.fori_loop(0, rows, body, 0, unroll=2)


def pack(arrive, lines, state, wetness, choice):
    n, width, nz = state.shape
    steps = 4
    return pl.pallas_call(
        pack_kernel,
        grid=(steps,),
        in_specs=[smem_spec(), smem_spec()] + dense(3),
        out_specs=[
            pl.BlockSpec((n // steps, count * width, nz), lambda i: (i, 0, 0))
            for count in (FAR, 5 - FAR)
            if count
        ],
        out_shape=[hbm(n, FAR * width, nz)] + [f32(n, (5 - FAR) * width, nz)] * (FAR < 5),
        compiler_params=limit(6),
        cost_estimate=cost(80 * n * width * nz, 9 * MIB),
        name="pack",
    )(arrive, lines, state, wetness, choice)


def thermal_kernel(p_hbm, far_hbm, *refs):
    near_refs, (send_hbm, p_ref, far_ref, send_ref, in_sem, out_sem) = refs[:-6], refs[-6:]
    n, width, nz = p_ref.shape
    chunks = in_sem.shape[1]
    size = n // chunks
    loads = copies([p_hbm, far_hbm], [p_ref, far_ref], in_sem, chunks)
    stores = copies([send_ref], [send_hbm], out_sem, chunks)
    for group in loads:
        for move in group:
            move.start()

    def body(s, carry):
        kept = [far_ref[s, k * width : (k + 1) * width, :] for k in range(FAR)]
        kept += [near_refs[0][s, k * width : (k + 1) * width, :] for k in range(5 - FAR)]
        heated = kept[0] + 0.5 * p_ref[s]
        share = jnp.exp(-2.0 * jnp.maximum(heated - 1.0, 0.0))
        send_ref[s, 0:width, :] = kept[1] + kept[2] * share
        send_ref[s, width : 2 * width, :] = kept[3] + kept[4] * share
        return carry

    for chunk in range(chunks):
        for move in loads[chunk]:
            move.wait()
        lax.fori_loop(chunk * size, (chunk + 1) * size, body, 0, unroll=4)
        for move in stores[chunk]:
            move.start()
    for group in stores:
        for move in group:
            move.wait()


def thermal(power, far, *near):
    n, width, nz = power.shape
    chunks = 8
    return pl.pallas_call(
        thermal_kernel,
        in_specs=[hbm_spec(), hbm_spec()] + dense(len(near)),
        out_specs=hbm_spec(),
        out_shape=hbm(n, 2 * width, nz),
        scratch_shapes=[
            pltpu.VMEM((n, width, nz), jnp.float32),
            pltpu.VMEM(far.shape, jnp.float32),
            pltpu.VMEM((n, 2 * width, nz), jnp.float32),
            pltpu.SemaphoreType.DMA((2, chunks)),
            pltpu.SemaphoreType.DMA((1, chunks)),
        ],
        compiler_params=limit(THERMAL_MIB),
        cost_estimate=cost(40 * n * width * nz, 8 * MIB),
        name="thermal",
    )(power, far, *near)


def heat_kernel(arrive, p_ref, t_ref, w_ref, t_out, w_out):
    n, width, nz = p_ref.shape
    lane = lax.broadcasted_iota(jnp.int32, (width, nz), 1)

    def body(s, carry):
        slot = arrive[0, s]
        state = t_ref[slot]
        above = jnp.where(lane == nz - 1, state, pltpu.roll(state, nz - 1, 1))
        below = jnp.where(lane == 0, state, pltpu.roll(state, 1, 1))
        heated = state + 0.2 * ((above - state) + (below - state)) + 0.5 * p_ref[s]
        wet = w_ref[slot]
        gone = wet * (1.0 - jnp.exp(-2.0 * jnp.maximum(heated - 1.0, 0.0)))
        w_out[slot] = wet - gone
        t_out[slot] = heated - 0.8 * gone
        return carry

    lax.fori_loop(0, n, body, 0, unroll=4)


def heat(arrive, power, state, wetness):
    n, width, nz = power.shape
    return pl.pallas_call(
        heat_kernel,
        in_specs=[smem_spec()] + dense(3),
        out_specs=dense(2),
        out_shape=[f32(n, width, nz)] * 2,
        compiler_params=limit(8),
        cost_estimate=cost(40 * n * width * nz, 5 * MIB),
        name="heat",
    )(arrive, power, state, wetness)


def near_kernel(eps_ref, sig_ref, lab_ref, out_ref):
    out_ref[0] = jnp.where(lab_ref[...] == 2, -1.0, eps_ref[...])
    out_ref[1] = sig_ref[...]


def near(eps, sig, label):
    nx, ny, nz = eps.shape
    steps = 4
    cells = pl.BlockSpec((nx // steps, ny, nz), lambda i: (i, 0, 0))
    return pl.pallas_call(
        near_kernel,
        grid=(steps,),
        in_specs=[cells] * 3,
        out_specs=pl.BlockSpec((2, nx // steps, ny, nz), lambda i: (0, i, 0, 0)),
        out_shape=f32(2, nx, ny, nz),
        compiler_params=limit(4),
        cost_estimate=cost(2 * nx * ny * nz, 5 * MIB),
        name="near",
    )(eps, sig, label)


def select_kernel(dest, recv_hbm, kept, eps_out, sig_out, recv, eps_new, sig_new, recv_sem, out_sem):
    nx, ny, nz = eps_new.shape
    parts = ny // 8
    chunks = out_sem.shape[1]
    size = nx // chunks
    group = size * parts
    stores = copies([eps_new, sig_new], [eps_out, sig_out], out_sem, chunks)

    for chunk in range(chunks):

        def fetch(k, carry, chunk=chunk):
            pltpu.make_async_copy(recv_hbm.at[dest[0, k]], recv.at[k], recv_sem.at[chunk]).start()
            return carry

        lax.fori_loop(chunk * group, (chunk + 1) * group, fetch, 0, unroll=8)

    def body(x, carry):
        for part in range(parts):
            rows = slice(part * 8, part * 8 + 8)
            eps = kept[0, x, rows, :]
            product = eps < 0.0
            eps_new[x, rows, :] = jnp.where(product, recv[x * parts + part, 0:8, :], eps)
            sig_new[x, rows, :] = jnp.where(product, recv[x * parts + part, 8:16, :], kept[1, x, rows, :])
        return carry

    for chunk in range(chunks):
        block = pl.ds(chunk * group, group)
        pltpu.make_async_copy(recv_hbm.at[block], recv.at[block], recv_sem.at[chunk]).wait()
        lax.fori_loop(chunk * size, (chunk + 1) * size, body, 0, unroll=2)
        for move in stores[chunk]:
            move.start()
    for moves in stores:
        for move in moves:
            move.wait()


def select(dest, recv, kept):
    nx, ny, nz = kept.shape[1:]
    chunks = 8
    cells = pltpu.VMEM((nx, ny, nz), jnp.float32)
    return pl.pallas_call(
        select_kernel,
        in_specs=[smem_spec(), hbm_spec(), vmem_spec()],
        out_specs=[hbm_spec()] * 2,
        out_shape=[hbm(nx, ny, nz), hbm(nx, ny, nz)],
        scratch_shapes=[
            pltpu.VMEM(recv.shape, jnp.float32),
            cells,
            cells,
            pltpu.SemaphoreType.DMA((chunks,)),
            pltpu.SemaphoreType.DMA((2, chunks)),
        ],
        compiler_params=limit(8),
        cost_estimate=cost(4 * nx * ny * nz, 7 * MIB),
        name="select",
    )(dest, recv, kept)


def exchange(value):
    return lax.all_to_all(value, ("gx", "gy"), split_axis=0, concat_axis=0, tiled=True)


def borders(layer, rows, by):
    return passed_along(layer, "gx", by), passed_along(rows, "gy", by)


def local(
    efield_vector,
    hfield_vector,
    dielectric_grid,
    sigma_grid,
    substance_label,
    thermal_state,
    wetness_share,
    dielectric_line_choice,
    dielectric_lookup_lines,
    dispatch_keeper_map,
    arrival_position_map,
):
    efield, hfield = efield_vector, hfield_vector
    e_fix, h_fix = (), ()
    layer, rows = first_halo(efield)
    for step in range(2):
        gx, gy = borders(layer, rows, -1)
        hfield, layer, rows, *h_kept = h_update(efield, e_fix, hfield, h_fix)
        h_fix = h_border(layer, rows, gx, gy)
        gx, gy = borders(*h_fix, 1)
        final = step == 1
        efield, layer, rows, *power = e_update(
            efield, e_fix, hfield, h_fix, dielectric_grid, sigma_grid, final
        )
        if final:
            power, *e_fix, e_kept = power_border(
                dispatch_keeper_map, efield, power[0], layer, rows, gx, gy
            )
        else:
            e_fix = layer, rows = e_border(layer, rows, gx, gy)
    arrived = exchange(power)
    blocks = lax.optimization_barrier(
        (power, thermal_state, wetness_share, dielectric_line_choice)
    )
    packed = pack(arrival_position_map, dielectric_lookup_lines, *blocks[1:])
    outgoing = thermal(arrived, *packed)
    returned = exchange(outgoing)
    outgoing, arrived, efield, hfield, label = lax.optimization_barrier(
        (outgoing, arrived, e_kept, h_kept[0], substance_label)
    )
    kept = near(dielectric_grid, sigma_grid, label)
    final_efield, final_hfield = flush(efield, e_fix, hfield, h_fix)
    warmth, moisture = heat(arrival_position_map, arrived, thermal_state, wetness_share)
    dielectric_result, sigma_result = select(
        dispatch_keeper_map, returned, kept
    )
    return final_efield, final_hfield, dielectric_result, sigma_result, warmth, moisture


def solution(mesh):
    in_specs = (
        P(None, "gx", "gy", None),
        P(None, "gx", "gy", None),
        P("gx", "gy", None),
        P("gx", "gy", None),
        P("gx", "gy", None),
        P(("gx", "gy"), None, None),
        P(("gx", "gy"), None, None),
        P(("gx", "gy"), None, None),
        P(),
        P(("gx", "gy"), None),
        P(("gx", "gy"), None),
    )
    out_specs = (
        P(None, "gx", "gy", None),
        P(None, "gx", "gy", None),
        P("gx", "gy", None),
        P("gx", "gy", None),
        P(("gx", "gy"), None, None),
        P(("gx", "gy"), None, None),
    )
    return jax.shard_map(local, mesh=mesh, in_specs=in_specs, out_specs=out_specs, check_vma=False)
```

```python
import functools

import jax
import jax.numpy as jnp
from jax import lax
from jax.experimental import pallas as pl
from jax.experimental.pallas import tpu as pltpu
from jax.sharding import PartitionSpec as P

DT = 0.5
MIB = 1 << 20
GROUP = 10
HALF = 5
FAR = 5
THERMAL_MIB = 62


def passed_along(value, axis, by):
    count = lax.axis_size(axis)
    pairs = [(i, i + by) for i in range(count) if 0 <= i + by < count]
    return lax.ppermute(value, axis, pairs)


def vmem_spec():
    return pl.BlockSpec(memory_space=pltpu.VMEM)


def smem_spec():
    return pl.BlockSpec(memory_space=pltpu.SMEM)


def f32(*shape):
    return jax.ShapeDtypeStruct(shape, jnp.float32)


def dense(count):
    return [vmem_spec()] * count


def limit(mib):
    return pltpu.CompilerParams(vmem_limit_bytes=mib * MIB)


def hbm_spec():
    return pl.BlockSpec(memory_space=pltpu.HBM)


def part_of(ref, axis, chunk, chunks):
    size = ref.shape[axis] // chunks
    where = [slice(None)] * axis + [pl.ds(chunk * size, size)]
    return ref.at[tuple(where)]


def copies(sources, targets, sem, chunks, axis=0):
    return [
        [
            pltpu.make_async_copy(
                part_of(source, axis, chunk, chunks), part_of(target, axis, chunk, chunks), sem.at[k, chunk]
            )
            for k, (source, target) in enumerate(zip(sources, targets))
        ]
        for chunk in range(chunks)
    ]


def hbm(*shape):
    return pltpu.HBM(shape, jnp.float32)


def cost(ops, nbytes):
    return pl.CostEstimate(flops=ops, bytes_accessed=nbytes, transcendentals=0)


def halo_kernel(layer_ref, e_ref, sx_ref, sy_ref):
    sx_ref[0] = layer_ref[1, 0]
    sx_ref[1] = layer_ref[2, 0]
    for x in range(e_ref.shape[1]):
        sy_ref[0, x : x + 1, :] = e_ref[0, x, 0:1, :]
        sy_ref[1, x : x + 1, :] = e_ref[2, x, 0:1, :]


def first_halo(efield):
    _, nx, ny, nz = efield.shape
    return pl.pallas_call(
        halo_kernel,
        grid=(1,),
        in_specs=[
            pl.BlockSpec((3, 1, ny, nz), lambda i: (0, 0, 0, 0)),
            pl.BlockSpec((3, nx, 8, nz), lambda i: (0, 0, 0, 0)),
        ],
        out_specs=[vmem_spec(), vmem_spec()],
        out_shape=[f32(2, ny, nz), f32(2, nx, nz)],
        compiler_params=limit(4),
        name="halo",
    )(efield, efield)


def patch_last(value, row):
    ny, nz = value.shape
    at = lax.broadcasted_iota(jnp.int32, (8, nz), 0) == 7
    return jnp.concatenate([value[: ny - 8], jnp.where(at, row, value[ny - 8 :])], axis=0)


def patch_first(value, row):
    nz = value.shape[1]
    at = lax.broadcasted_iota(jnp.int32, (8, nz), 0) == 0
    return jnp.concatenate([jnp.where(at, row, value[:8]), value[8:]], axis=0)


def fwd_z(f):
    ny, nz = f.shape
    lane = lax.broadcasted_iota(jnp.int32, f.shape, 1)
    return jnp.where(lane == nz - 1, 0.0, pltpu.roll(f, nz - 1, 1)) - f


def bwd_z(f):
    lane = lax.broadcasted_iota(jnp.int32, f.shape, 1)
    return f - jnp.where(lane == 0, 0.0, pltpu.roll(f, 1, 1))


def fwd_y(f):
    ny = f.shape[0]
    return patch_last(pltpu.roll(f, ny - 1, 0), 0.0) - f


def bwd_y(f):
    return f - patch_first(pltpu.roll(f, 1, 0), 0.0)


def e_slab(x, first, e_ref, layer_ref, rows_ref):
    ex, ey, ez = e_ref[0, x], e_ref[1, x], e_ref[2, x]
    if rows_ref is not None:
        ex = patch_first(ex, rows_ref[0, pl.ds(x, 1), :])
        if first:
            ey, ez = layer_ref[0], layer_ref[1]
        else:
            ez = patch_first(ez, rows_ref[1, pl.ds(x, 1), :])
    return ex, ey, ez


def h_slab(x, last, h_ref, layer_ref, rows_ref):
    hx, hy, hz = h_ref[0, x], h_ref[1, x], h_ref[2, x]
    if rows_ref is not None:
        hx = patch_last(hx, rows_ref[0, pl.ds(x, 1), :])
        if last:
            hy, hz = layer_ref[0], layer_ref[1]
        else:
            hz = patch_last(hz, rows_ref[1, pl.ds(x, 1), :])
    return hx, hy, hz


def walk(slab, nx, move=None):
    groups = (nx - 2) // GROUP
    pieces = GROUP // HALF

    def send(*where):
        if move is not None:
            move(*where).start()

    slab(0, True, False)
    send(0, 1, 0)

    def body(g, carry):
        for piece in range(pieces):
            first = 1 + g * GROUP + piece * HALF
            for k in range(HALF):
                slab(first + k, False, False)
            send(first, HALF, 1 + g * pieces + piece)
        return carry

    lax.fori_loop(0, groups, body, 0)
    for x in range(1 + groups * GROUP, nx - 1):
        slab(x, False, False)
    slab(nx - 1, False, True)
    rest = 1 + groups * GROUP
    send(rest, nx - rest, 1 + groups * pieces)
    if move is not None:
        move(0, 1, 0).wait()
        for k in range(groups * pieces):
            move(1 + k * HALF, HALF, 1 + k).wait()
        move(rest, nx - rest, 1 + groups * pieces).wait()


def carry_off(source, target, sem):
    def move(start, size, index):
        where = (slice(None), pl.ds(start, size))
        return pltpu.make_async_copy(source.at[where], target.at[where], sem.at[index])

    return move


def copy_count(nx):
    return 2 + (nx - 2) // GROUP * (GROUP // HALF)


def h_kernel(fixed, *refs):
    if fixed:
        e_ref, el_ref, er_ref, h_ref, hl_ref, hr_ref, out_ref, layer_ref, rows_ref, out_hbm, sem = refs
    else:
        e_ref, h_ref, out_ref, layer_ref, rows_ref = refs
        el_ref = er_ref = hl_ref = hr_ref = None
    nx, ny, nz = e_ref.shape[1:]

    def slab(x, first, last):
        ex, ey, ez = e_slab(x, first, e_ref, el_ref, er_ref)
        hx, hy, hz = h_slab(x, last, h_ref, hl_ref, hr_ref)
        if last:
            ey_step, ez_step = -ey, -ez
        else:
            _, ey_next, ez_next = e_slab(x + 1, False, e_ref, el_ref, er_ref)
            ey_step, ez_step = ey_next - ey, ez_next - ez
        hx = hx - DT * (fwd_y(ez) - fwd_z(ey))
        hy = hy - DT * (fwd_z(ex) - ez_step)
        hz = hz - DT * (ey_step - fwd_y(ex))
        out_ref[0, x] = hx
        out_ref[1, x] = hy
        out_ref[2, x] = hz
        rows_ref[0, pl.ds(x, 1), :] = hx[ny - 1 : ny]
        rows_ref[1, pl.ds(x, 1), :] = hz[ny - 1 : ny]
        if last:
            layer_ref[0] = hy
            layer_ref[1] = hz

    walk(slab, nx, carry_off(out_ref, out_hbm, sem) if fixed else None)


def h_update(efield, e_fix, hfield, h_fix):
    _, nx, ny, nz = efield.shape
    args = [efield, *e_fix, hfield, *h_fix]
    outs = [f32(3, nx, ny, nz), f32(2, ny, nz), f32(2, nx, nz)]
    return pl.pallas_call(
        functools.partial(h_kernel, bool(e_fix)),
        in_specs=dense(len(args)),
        out_specs=dense(3) + [hbm_spec()] * bool(e_fix),
        out_shape=outs + [hbm(3, nx, ny, nz)] * bool(e_fix),
        scratch_shapes=[pltpu.SemaphoreType.DMA((copy_count(nx),))] * bool(e_fix),
        compiler_params=limit(16),
        cost_estimate=cost(40 * nx * ny * nz, 9 * MIB),
        name="hstep",
    )(*args)


def h_border_kernel(layer_ref, rows_ref, gx_ref, gy_ref, layer_out, rows_out):
    ny, nx = layer_ref.shape[1], rows_ref.shape[1]
    layer_out[0] = layer_ref[0] + DT * gx_ref[1]
    layer_out[1] = patch_last(
        layer_ref[1] - DT * gx_ref[0],
        layer_ref[1, ny - 1 : ny] - DT * gx_ref[0, ny - 1 : ny] + DT * gy_ref[0, nx - 1 : nx],
    )
    rows_out[0] = rows_ref[0] - DT * gy_ref[1]
    rows_out[1] = patch_last(
        rows_ref[1] + DT * gy_ref[0],
        rows_ref[1, nx - 1 : nx] - DT * gx_ref[0, ny - 1 : ny] + DT * gy_ref[0, nx - 1 : nx],
    )


def h_border(layer, rows, gx, gy):
    return pl.pallas_call(
        h_border_kernel,
        in_specs=dense(4),
        out_specs=dense(2),
        out_shape=[f32(*layer.shape), f32(*rows.shape)],
        compiler_params=limit(2),
        name="hborder",
    )(layer, rows, gx, gy)


def e_kernel(fixed, final, *refs):
    refs = list(refs)
    if final:
        *refs, keep_ref, sem = refs
    e_ref = refs.pop(0)
    el_ref, er_ref = (refs.pop(0), refs.pop(0)) if fixed else (None, None)
    h_ref, hl_ref, hr_ref, eps_ref, sig_ref, out_ref, layer_ref, rows_ref = refs[:8]
    nx, ny, nz = e_ref.shape[1:]
    move = None
    if final:
        move = carry_off(keep_ref, out_ref, sem)
        out_ref = keep_ref

    def slab(x, first, last):
        hx, hy, hz = h_slab(x, last, h_ref, hl_ref, hr_ref)
        if first:
            hy_step, hz_step = hy, hz
        else:
            _, hy_prev, hz_prev = h_slab(x - 1, False, h_ref, hl_ref, hr_ref)
            hy_step, hz_step = hy - hy_prev, hz - hz_prev
        sig = sig_ref[x]
        quarter = 0.25 * sig
        eps = eps_ref[x]
        inv = 1.0 / (eps + quarter)
        scale_e = (eps - quarter) * inv
        scale_c = DT * inv
        ex0, ey0, ez0 = e_slab(x, first, e_ref, el_ref, er_ref)
        ex = scale_e * ex0 + scale_c * (bwd_y(hz) - bwd_z(hy))
        ey = scale_e * ey0 + scale_c * (bwd_z(hx) - hz_step)
        ez = scale_e * ez0 + scale_c * (hy_step - bwd_y(hx))
        out_ref[0, x] = ex
        out_ref[1, x] = ey
        out_ref[2, x] = ez
        at = pl.ds(x, 1)
        rows_ref[0, at, :] = ex[0:1]
        rows_ref[1, at, :] = ez[0:1]
        rows_ref[2, at, :] = scale_c[0:1]
        if first:
            layer_ref[0] = ey
            layer_ref[1] = ez
            layer_ref[2] = scale_c
        if final:
            before = ex0 * ex0 + ey0 * ey0 + ez0 * ez0
            half = 0.5 * sig
            refs[8][x] = half * (before + (ex * ex + ey * ey + ez * ez))
            rows_ref[3, at, :] = ey[0:1]
            rows_ref[4, at, :] = before[0:1]
            rows_ref[5, at, :] = half[0:1]
            if first:
                layer_ref[3] = ex
                layer_ref[4] = before
                layer_ref[5] = half

    walk(slab, nx, move)


def e_update(efield, e_fix, hfield, h_fix, eps, sig, final):
    _, nx, ny, nz = efield.shape
    args = [efield, *e_fix, hfield, *h_fix, eps, sig]
    kept = 6 if final else 3
    outs = [f32(3, nx, ny, nz), f32(kept, ny, nz), f32(kept, nx, nz)]
    specs = dense(3)
    scratch = []
    if final:
        outs[0] = hbm(3, nx, ny, nz)
        outs.append(f32(nx, ny, nz))
        specs = [hbm_spec(), vmem_spec(), vmem_spec(), vmem_spec()]
        scratch = [pltpu.VMEM((3, nx, ny, nz), jnp.float32), pltpu.SemaphoreType.DMA((copy_count(nx),))]
    return pl.pallas_call(
        functools.partial(e_kernel, bool(e_fix), final),
        in_specs=dense(len(args)),
        out_specs=specs,
        out_shape=outs,
        scratch_shapes=scratch,
        compiler_params=limit(16),
        cost_estimate=cost(60 * nx * ny * nz, 11 * MIB),
        name="estep",
    )(*args)


def e_border_values(layer_ref, rows_ref, gx_ref, gy_ref):
    ey_layer = layer_ref[0] + layer_ref[2] * gx_ref[1]
    ez_layer = layer_ref[1] - layer_ref[2] * gx_ref[0]
    ez_layer = patch_first(ez_layer, ez_layer[0:1] + layer_ref[2, 0:1] * gy_ref[0, 0:1])
    ex_rows = rows_ref[0] - rows_ref[2] * gy_ref[1]
    ez_rows = patch_first(rows_ref[1] + rows_ref[2] * gy_ref[0], ez_layer[0:1])
    return ey_layer, ez_layer, ex_rows, ez_rows


def e_border_kernel(layer_ref, rows_ref, gx_ref, gy_ref, layer_out, rows_out):
    layer_out[0], layer_out[1], rows_out[0], rows_out[1] = e_border_values(
        layer_ref, rows_ref, gx_ref, gy_ref
    )


def e_border(layer, rows, gx, gy):
    return pl.pallas_call(
        e_border_kernel,
        in_specs=dense(4),
        out_specs=dense(2),
        out_shape=[f32(*gx.shape), f32(*gy.shape)],
        compiler_params=limit(2),
        name="eborder",
    )(layer, rows, gx, gy)


def power_kernel(dest, p_ref, layer_ref, rows_ref, gx_ref, gy_ref, out_hbm, layer_out, rows_out, scratch, out_ref, sem):
    nx, ny, nz = p_ref.shape
    parts = ny // 8
    ey_layer, ez_layer, ex_rows, ez_rows = e_border_values(layer_ref, rows_ref, gx_ref, gy_ref)
    layer_out[0], layer_out[1], rows_out[0], rows_out[1] = ey_layer, ez_layer, ex_rows, ez_rows
    ex_layer = patch_first(layer_ref[3], ex_rows[0:1])
    squares = ex_layer * ex_layer + ey_layer * ey_layer + ez_layer * ez_layer
    layer_power = layer_ref[5] * (layer_ref[4] + squares)
    ey_rows = rows_ref[3]
    squares = ex_rows * ex_rows + ey_rows * ey_rows + ez_rows * ez_rows
    scratch[...] = rows_ref[5] * (rows_ref[4] + squares)
    top = lax.broadcasted_iota(jnp.int32, (8, nz), 0) == 0

    for part in range(parts):
        out_ref[dest[0, part]] = layer_power[part * 8 : part * 8 + 8]

    def body(x, carry):
        row = scratch[pl.ds(x, 1), :]
        out_ref[dest[0, x * parts]] = jnp.where(top, row, p_ref[x, 0:8, :])
        for part in range(1, parts):
            out_ref[dest[0, x * parts + part]] = p_ref[x, part * 8 : part * 8 + 8, :]
        return carry

    lax.fori_loop(1, nx, body, 0, unroll=2)
    move = pltpu.make_async_copy(out_ref, out_hbm, sem)
    move.start()
    move.wait()


def power_border(dest, power, layer, rows, gx, gy):
    nx, ny, nz = power.shape
    return pl.pallas_call(
        power_kernel,
        in_specs=[smem_spec()] + dense(5),
        out_specs=[hbm_spec()] + dense(2),
        out_shape=[hbm(nx * ny // 8, 8, nz), f32(*gx.shape), f32(*gy.shape)],
        scratch_shapes=[
            pltpu.VMEM((nx, nz), jnp.float32),
            pltpu.VMEM((nx * ny // 8, 8, nz), jnp.float32),
            pltpu.SemaphoreType.DMA(()),
        ],
        compiler_params=limit(8),
        cost_estimate=cost(4 * nx * ny * nz, 2 * MIB),
        name="power",
    )(dest, power, layer, rows, gx, gy)


def flush_kernel(e_ref, el_ref, er_ref, h_ref, hl_ref, hr_ref, e_out, h_out):
    nx = e_ref.shape[1]

    def slab(x, first, last):
        e_out[0, x], e_out[1, x], e_out[2, x] = e_slab(x, first, e_ref, el_ref, er_ref)
        h_out[0, x], h_out[1, x], h_out[2, x] = h_slab(x, last, h_ref, hl_ref, hr_ref)

    slab(0, True, False)
    lax.fori_loop(1, nx - 1, lambda x, c: (slab(x, False, False), c)[1], 0)
    slab(nx - 1, False, True)


def flush(efield, e_fix, hfield, h_fix):
    return pl.pallas_call(
        flush_kernel,
        in_specs=dense(6),
        out_specs=dense(2),
        out_shape=[f32(*efield.shape), f32(*hfield.shape)],
        compiler_params=limit(16),
        cost_estimate=cost(efield.size, 12 * MIB),
        name="flush",
    )(efield, *e_fix, hfield, *h_fix)


def pack_kernel(arrive, lines, t_ref, w_ref, c_ref, *out_refs):
    rows = out_refs[0].shape[0]
    width, nz = t_ref.shape[1:]
    levels = lines.shape[1]
    step = pl.program_id(0)
    lane = lax.broadcasted_iota(jnp.int32, (width, nz), 1)

    def body(r, carry):
        slot = arrive[0, step * rows + r]
        state = t_ref[slot]
        choice = c_ref[slot]
        above = jnp.where(lane == nz - 1, state, pltpu.roll(state, nz - 1, 1))
        below = jnp.where(lane == 0, state, pltpu.roll(state, 1, 1))
        factors = [jnp.full(choice.shape, lines[c, 0], jnp.float32) for c in range(4)]
        for level in range(1, levels):
            match = choice == level
            for c in range(4):
                factors[c] = jnp.where(match, lines[c, level], factors[c])
        wet = w_ref[slot]
        values = [
            state + 0.2 * ((above - state) + (below - state)),
            1.0 + factors[0],
            4.0 * factors[1] * wet,
            0.1 * factors[2],
            0.3 * factors[3] * wet,
        ]
        for k, value in enumerate(values):
            target, at = (out_refs[0], k) if k < FAR else (out_refs[1], k - FAR)
            target[r, at * width : (at + 1) * width, :] = value
        return carry

    lax.fori_loop(0, rows, body, 0, unroll=2)


def pack(arrive, lines, state, wetness, choice):
    n, width, nz = state.shape
    steps = 4
    return pl.pallas_call(
        pack_kernel,
        grid=(steps,),
        in_specs=[smem_spec(), smem_spec()] + dense(3),
        out_specs=[
            pl.BlockSpec((n // steps, count * width, nz), lambda i: (i, 0, 0))
            for count in (FAR, 5 - FAR)
            if count
        ],
        out_shape=[hbm(n, FAR * width, nz)] + [f32(n, (5 - FAR) * width, nz)] * (FAR < 5),
        compiler_params=limit(6),
        cost_estimate=cost(80 * n * width * nz, 9 * MIB),
        name="pack",
    )(arrive, lines, state, wetness, choice)


def thermal_kernel(p_hbm, far_hbm, *refs):
    near_refs, (send_hbm, p_ref, far_ref, send_ref, in_sem, out_sem) = refs[:-6], refs[-6:]
    n, width, nz = p_ref.shape
    chunks = in_sem.shape[1]
    size = n // chunks
    loads = copies([p_hbm, far_hbm], [p_ref, far_ref], in_sem, chunks)
    stores = copies([send_ref], [send_hbm], out_sem, chunks)
    for group in loads:
        for move in group:
            move.start()

    def body(s, carry):
        kept = [far_ref[s, k * width : (k + 1) * width, :] for k in range(FAR)]
        kept += [near_refs[0][s, k * width : (k + 1) * width, :] for k in range(5 - FAR)]
        heated = kept[0] + 0.5 * p_ref[s]
        share = jnp.exp(-2.0 * jnp.maximum(heated - 1.0, 0.0))
        send_ref[s, 0:width, :] = kept[1] + kept[2] * share
        send_ref[s, width : 2 * width, :] = kept[3] + kept[4] * share
        return carry

    for chunk in range(chunks):
        for move in loads[chunk]:
            move.wait()
        lax.fori_loop(chunk * size, (chunk + 1) * size, body, 0, unroll=4)
        for move in stores[chunk]:
            move.start()
    for group in stores:
        for move in group:
            move.wait()


def thermal(power, far, *near):
    n, width, nz = power.shape
    chunks = 8
    return pl.pallas_call(
        thermal_kernel,
        in_specs=[hbm_spec(), hbm_spec()] + dense(len(near)),
        out_specs=hbm_spec(),
        out_shape=hbm(n, 2 * width, nz),
        scratch_shapes=[
            pltpu.VMEM((n, width, nz), jnp.float32),
            pltpu.VMEM(far.shape, jnp.float32),
            pltpu.VMEM((n, 2 * width, nz), jnp.float32),
            pltpu.SemaphoreType.DMA((2, chunks)),
            pltpu.SemaphoreType.DMA((1, chunks)),
        ],
        compiler_params=limit(THERMAL_MIB),
        cost_estimate=cost(40 * n * width * nz, 8 * MIB),
        name="thermal",
    )(power, far, *near)


def heat_kernel(arrive, p_ref, t_ref, w_ref, t_out, w_out):
    n, width, nz = p_ref.shape
    lane = lax.broadcasted_iota(jnp.int32, (width, nz), 1)

    def body(s, carry):
        slot = arrive[0, s]
        state = t_ref[slot]
        above = jnp.where(lane == nz - 1, state, pltpu.roll(state, nz - 1, 1))
        below = jnp.where(lane == 0, state, pltpu.roll(state, 1, 1))
        heated = state + 0.2 * ((above - state) + (below - state)) + 0.5 * p_ref[s]
        wet = w_ref[slot]
        gone = wet * (1.0 - jnp.exp(-2.0 * jnp.maximum(heated - 1.0, 0.0)))
        w_out[slot] = wet - gone
        t_out[slot] = heated - 0.8 * gone
        return carry

    lax.fori_loop(0, n, body, 0, unroll=4)


def heat(arrive, power, state, wetness):
    n, width, nz = power.shape
    return pl.pallas_call(
        heat_kernel,
        in_specs=[smem_spec()] + dense(3),
        out_specs=dense(2),
        out_shape=[f32(n, width, nz)] * 2,
        compiler_params=limit(8),
        cost_estimate=cost(40 * n * width * nz, 5 * MIB),
        name="heat",
    )(arrive, power, state, wetness)


def near_kernel(eps_ref, sig_ref, lab_ref, out_ref):
    out_ref[0] = jnp.where(lab_ref[...] == 2, -1.0, eps_ref[...])
    out_ref[1] = sig_ref[...]


def near(eps, sig, label):
    nx, ny, nz = eps.shape
    steps = 4
    cells = pl.BlockSpec((nx // steps, ny, nz), lambda i: (i, 0, 0))
    return pl.pallas_call(
        near_kernel,
        grid=(steps,),
        in_specs=[cells] * 3,
        out_specs=pl.BlockSpec((2, nx // steps, ny, nz), lambda i: (0, i, 0, 0)),
        out_shape=f32(2, nx, ny, nz),
        compiler_params=limit(4),
        cost_estimate=cost(2 * nx * ny * nz, 5 * MIB),
        name="near",
    )(eps, sig, label)


def select_kernel(dest, recv_hbm, kept, eps_out, sig_out, recv, eps_new, sig_new, recv_sem, out_sem):
    nx, ny, nz = eps_new.shape
    parts = ny // 8
    chunks = out_sem.shape[1]
    size = nx // chunks
    group = size * parts
    stores = copies([eps_new, sig_new], [eps_out, sig_out], out_sem, chunks)

    for chunk in range(chunks):

        def fetch(k, carry, chunk=chunk):
            pltpu.make_async_copy(recv_hbm.at[dest[0, k]], recv.at[k], recv_sem.at[chunk]).start()
            return carry

        lax.fori_loop(chunk * group, (chunk + 1) * group, fetch, 0, unroll=8)

    def body(x, carry):
        for part in range(parts):
            rows = slice(part * 8, part * 8 + 8)
            eps = kept[0, x, rows, :]
            product = eps < 0.0
            eps_new[x, rows, :] = jnp.where(product, recv[x * parts + part, 0:8, :], eps)
            sig_new[x, rows, :] = jnp.where(product, recv[x * parts + part, 8:16, :], kept[1, x, rows, :])
        return carry

    for chunk in range(chunks):
        block = pl.ds(chunk * group, group)
        pltpu.make_async_copy(recv_hbm.at[block], recv.at[block], recv_sem.at[chunk]).wait()
        lax.fori_loop(chunk * size, (chunk + 1) * size, body, 0, unroll=2)
        for move in stores[chunk]:
            move.start()
    for moves in stores:
        for move in moves:
            move.wait()


def select(dest, recv, kept):
    nx, ny, nz = kept.shape[1:]
    chunks = 8
    cells = pltpu.VMEM((nx, ny, nz), jnp.float32)
    return pl.pallas_call(
        select_kernel,
        in_specs=[smem_spec(), hbm_spec(), vmem_spec()],
        out_specs=[hbm_spec()] * 2,
        out_shape=[hbm(nx, ny, nz), hbm(nx, ny, nz)],
        scratch_shapes=[
            pltpu.VMEM(recv.shape, jnp.float32),
            cells,
            cells,
            pltpu.SemaphoreType.DMA((chunks,)),
            pltpu.SemaphoreType.DMA((2, chunks)),
        ],
        compiler_params=limit(8),
        cost_estimate=cost(4 * nx * ny * nz, 7 * MIB),
        name="select",
    )(dest, recv, kept)


def exchange(value):
    return lax.all_to_all(value, ("gx", "gy"), split_axis=0, concat_axis=0, tiled=True)


def borders(layer, rows, by):
    return passed_along(layer, "gx", by), passed_along(rows, "gy", by)


def local(
    efield_vector,
    hfield_vector,
    dielectric_grid,
    sigma_grid,
    substance_label,
    thermal_state,
    wetness_share,
    dielectric_line_choice,
    dielectric_lookup_lines,
    dispatch_keeper_map,
    arrival_position_map,
):
    efield, hfield = efield_vector, hfield_vector
    e_fix, h_fix = (), ()
    layer, rows = first_halo(efield)
    for step in range(2):
        gx, gy = borders(layer, rows, -1)
        hfield, layer, rows, *h_kept = h_update(efield, e_fix, hfield, h_fix)
        h_fix = h_border(layer, rows, gx, gy)
        gx, gy = borders(*h_fix, 1)
        final = step == 1
        efield, layer, rows, *power = e_update(
            efield, e_fix, hfield, h_fix, dielectric_grid, sigma_grid, final
        )
        if final:
            power, *e_fix = power_border(dispatch_keeper_map, power[0], layer, rows, gx, gy)
        else:
            e_fix = layer, rows = e_border(layer, rows, gx, gy)
    arrived = exchange(power)
    blocks = lax.optimization_barrier(
        (power, thermal_state, wetness_share, dielectric_line_choice)
    )
    packed = pack(arrival_position_map, dielectric_lookup_lines, *blocks[1:])
    outgoing = thermal(arrived, *packed)
    returned = exchange(outgoing)
    outgoing, arrived, efield, hfield, label = lax.optimization_barrier(
        (outgoing, arrived, efield, h_kept[0], substance_label)
    )
    kept = near(dielectric_grid, sigma_grid, label)
    final_efield, final_hfield = flush(efield, e_fix, hfield, h_fix)
    warmth, moisture = heat(arrival_position_map, arrived, thermal_state, wetness_share)
    dielectric_result, sigma_result = select(
        dispatch_keeper_map, returned, kept
    )
    return final_efield, final_hfield, dielectric_result, sigma_result, warmth, moisture


def solution(mesh):
    in_specs = (
        P(None, "gx", "gy", None),
        P(None, "gx", "gy", None),
        P("gx", "gy", None),
        P("gx", "gy", None),
        P("gx", "gy", None),
        P(("gx", "gy"), None, None),
        P(("gx", "gy"), None, None),
        P(("gx", "gy"), None, None),
        P(),
        P(("gx", "gy"), None),
        P(("gx", "gy"), None),
    )
    out_specs = (
        P(None, "gx", "gy", None),
        P(None, "gx", "gy", None),
        P("gx", "gy", None),
        P("gx", "gy", None),
        P(("gx", "gy"), None, None),
        P(("gx", "gy"), None, None),
    )
    return jax.shard_map(local, mesh=mesh, in_specs=in_specs, out_specs=out_specs, check_vma=False)
```

```python
import functools

import jax
import jax.numpy as jnp
from jax import lax
from jax.experimental import pallas as pl
from jax.experimental.pallas import tpu as pltpu
from jax.sharding import PartitionSpec as P

DT = 0.5
MIB = 1 << 20
GROUP = 10
HALF = 5
FAR = 5
THERMAL_MIB = 62


def passed_along(value, axis, by):
    count = lax.axis_size(axis)
    pairs = [(i, i + by) for i in range(count) if 0 <= i + by < count]
    return lax.ppermute(value, axis, pairs)


def vmem_spec():
    return pl.BlockSpec(memory_space=pltpu.VMEM)


def smem_spec():
    return pl.BlockSpec(memory_space=pltpu.SMEM)


def f32(*shape):
    return jax.ShapeDtypeStruct(shape, jnp.float32)


def dense(count):
    return [vmem_spec()] * count


def limit(mib):
    return pltpu.CompilerParams(vmem_limit_bytes=mib * MIB)


def hbm_spec():
    return pl.BlockSpec(memory_space=pltpu.HBM)


def part_of(ref, axis, chunk, chunks):
    size = ref.shape[axis] // chunks
    where = [slice(None)] * axis + [pl.ds(chunk * size, size)]
    return ref.at[tuple(where)]


def copies(sources, targets, sem, chunks, axis=0):
    return [
        [
            pltpu.make_async_copy(
                part_of(source, axis, chunk, chunks), part_of(target, axis, chunk, chunks), sem.at[k, chunk]
            )
            for k, (source, target) in enumerate(zip(sources, targets))
        ]
        for chunk in range(chunks)
    ]


def hbm(*shape):
    return pltpu.HBM(shape, jnp.float32)


def cost(ops, nbytes):
    return pl.CostEstimate(flops=ops, bytes_accessed=nbytes, transcendentals=0)


def halo_kernel(layer_ref, e_ref, sx_ref, sy_ref):
    sx_ref[0] = layer_ref[1, 0]
    sx_ref[1] = layer_ref[2, 0]
    for x in range(e_ref.shape[1]):
        sy_ref[0, x : x + 1, :] = e_ref[0, x, 0:1, :]
        sy_ref[1, x : x + 1, :] = e_ref[2, x, 0:1, :]


def first_halo(efield):
    _, nx, ny, nz = efield.shape
    return pl.pallas_call(
        halo_kernel,
        grid=(1,),
        in_specs=[
            pl.BlockSpec((3, 1, ny, nz), lambda i: (0, 0, 0, 0)),
            pl.BlockSpec((3, nx, 8, nz), lambda i: (0, 0, 0, 0)),
        ],
        out_specs=[vmem_spec(), vmem_spec()],
        out_shape=[f32(2, ny, nz), f32(2, nx, nz)],
        compiler_params=limit(4),
        name="halo",
    )(efield, efield)


def patch_last(value, row):
    ny, nz = value.shape
    at = lax.broadcasted_iota(jnp.int32, (8, nz), 0) == 7
    return jnp.concatenate([value[: ny - 8], jnp.where(at, row, value[ny - 8 :])], axis=0)


def patch_first(value, row):
    nz = value.shape[1]
    at = lax.broadcasted_iota(jnp.int32, (8, nz), 0) == 0
    return jnp.concatenate([jnp.where(at, row, value[:8]), value[8:]], axis=0)


def fwd_z(f):
    ny, nz = f.shape
    lane = lax.broadcasted_iota(jnp.int32, f.shape, 1)
    return jnp.where(lane == nz - 1, 0.0, pltpu.roll(f, nz - 1, 1)) - f


def bwd_z(f):
    lane = lax.broadcasted_iota(jnp.int32, f.shape, 1)
    return f - jnp.where(lane == 0, 0.0, pltpu.roll(f, 1, 1))


def fwd_y(f):
    ny = f.shape[0]
    return patch_last(pltpu.roll(f, ny - 1, 0), 0.0) - f


def bwd_y(f):
    return f - patch_first(pltpu.roll(f, 1, 0), 0.0)


def e_slab(x, first, e_ref, layer_ref, rows_ref):
    ex, ey, ez = e_ref[0, x], e_ref[1, x], e_ref[2, x]
    if rows_ref is not None:
        ex = patch_first(ex, rows_ref[0, pl.ds(x, 1), :])
        if first:
            ey, ez = layer_ref[0], layer_ref[1]
        else:
            ez = patch_first(ez, rows_ref[1, pl.ds(x, 1), :])
    return ex, ey, ez


def h_slab(x, last, h_ref, layer_ref, rows_ref):
    hx, hy, hz = h_ref[0, x], h_ref[1, x], h_ref[2, x]
    if rows_ref is not None:
        hx = patch_last(hx, rows_ref[0, pl.ds(x, 1), :])
        if last:
            hy, hz = layer_ref[0], layer_ref[1]
        else:
            hz = patch_last(hz, rows_ref[1, pl.ds(x, 1), :])
    return hx, hy, hz


def walk(slab, nx, move=None):
    groups = (nx - 2) // GROUP
    pieces = GROUP // HALF

    def send(*where):
        if move is not None:
            move(*where).start()

    slab(0, True, False)
    send(0, 1, 0)

    def body(g, carry):
        for piece in range(pieces):
            first = 1 + g * GROUP + piece * HALF
            for k in range(HALF):
                slab(first + k, False, False)
            send(first, HALF, 1 + g * pieces + piece)
        return carry

    lax.fori_loop(0, groups, body, 0)
    for x in range(1 + groups * GROUP, nx - 1):
        slab(x, False, False)
    slab(nx - 1, False, True)
    rest = 1 + groups * GROUP
    send(rest, nx - rest, 1 + groups * pieces)
    if move is not None:
        move(0, 1, 0).wait()
        for k in range(groups * pieces):
            move(1 + k * HALF, HALF, 1 + k).wait()
        move(rest, nx - rest, 1 + groups * pieces).wait()


def carry_off(source, target, sem):
    def move(start, size, index):
        where = (slice(None), pl.ds(start, size))
        return pltpu.make_async_copy(source.at[where], target.at[where], sem.at[index])

    return move


def copy_count(nx):
    return 2 + (nx - 2) // GROUP * (GROUP // HALF)


def h_kernel(fixed, *refs):
    if fixed:
        e_ref, el_ref, er_ref, h_ref, hl_ref, hr_ref, out_ref, layer_ref, rows_ref, out_hbm, sem = refs
    else:
        e_ref, h_ref, out_ref, layer_ref, rows_ref = refs
        el_ref = er_ref = hl_ref = hr_ref = None
    nx, ny, nz = e_ref.shape[1:]

    def slab(x, first, last):
        ex, ey, ez = e_slab(x, first, e_ref, el_ref, er_ref)
        hx, hy, hz = h_slab(x, last, h_ref, hl_ref, hr_ref)
        if last:
            ey_step, ez_step = -ey, -ez
        else:
            _, ey_next, ez_next = e_slab(x + 1, False, e_ref, el_ref, er_ref)
            ey_step, ez_step = ey_next - ey, ez_next - ez
        hx = hx - DT * (fwd_y(ez) - fwd_z(ey))
        hy = hy - DT * (fwd_z(ex) - ez_step)
        hz = hz - DT * (ey_step - fwd_y(ex))
        out_ref[0, x] = hx
        out_ref[1, x] = hy
        out_ref[2, x] = hz
        rows_ref[0, pl.ds(x, 1), :] = hx[ny - 1 : ny]
        rows_ref[1, pl.ds(x, 1), :] = hz[ny - 1 : ny]
        if last:
            layer_ref[0] = hy
            layer_ref[1] = hz

    walk(slab, nx, carry_off(out_ref, out_hbm, sem) if fixed else None)


def h_update(efield, e_fix, hfield, h_fix):
    _, nx, ny, nz = efield.shape
    args = [efield, *e_fix, hfield, *h_fix]
    outs = [f32(3, nx, ny, nz), f32(2, ny, nz), f32(2, nx, nz)]
    return pl.pallas_call(
        functools.partial(h_kernel, bool(e_fix)),
        in_specs=dense(len(args)),
        out_specs=dense(3) + [hbm_spec()] * bool(e_fix),
        out_shape=outs + [hbm(3, nx, ny, nz)] * bool(e_fix),
        scratch_shapes=[pltpu.SemaphoreType.DMA((copy_count(nx),))] * bool(e_fix),
        compiler_params=limit(16),
        cost_estimate=cost(40 * nx * ny * nz, 9 * MIB),
        name="hstep",
    )(*args)


def h_border_kernel(layer_ref, rows_ref, gx_ref, gy_ref, layer_out, rows_out):
    ny, nx = layer_ref.shape[1], rows_ref.shape[1]
    layer_out[0] = layer_ref[0] + DT * gx_ref[1]
    layer_out[1] = patch_last(
        layer_ref[1] - DT * gx_ref[0],
        layer_ref[1, ny - 1 : ny] - DT * gx_ref[0, ny - 1 : ny] + DT * gy_ref[0, nx - 1 : nx],
    )
    rows_out[0] = rows_ref[0] - DT * gy_ref[1]
    rows_out[1] = patch_last(
        rows_ref[1] + DT * gy_ref[0],
        rows_ref[1, nx - 1 : nx] - DT * gx_ref[0, ny - 1 : ny] + DT * gy_ref[0, nx - 1 : nx],
    )


def h_border(layer, rows, gx, gy):
    return pl.pallas_call(
        h_border_kernel,
        in_specs=dense(4),
        out_specs=dense(2),
        out_shape=[f32(*layer.shape), f32(*rows.shape)],
        compiler_params=limit(2),
        name="hborder",
    )(layer, rows, gx, gy)


def e_kernel(fixed, final, *refs):
    refs = list(refs)
    if final:
        *refs, keep_ref, sem = refs
    e_ref = refs.pop(0)
    el_ref, er_ref = (refs.pop(0), refs.pop(0)) if fixed else (None, None)
    h_ref, hl_ref, hr_ref, eps_ref, sig_ref, out_ref, layer_ref, rows_ref = refs[:8]
    nx, ny, nz = e_ref.shape[1:]
    move = None
    if final:
        move = carry_off(keep_ref, out_ref, sem)
        out_ref = keep_ref

    def slab(x, first, last):
        hx, hy, hz = h_slab(x, last, h_ref, hl_ref, hr_ref)
        if first:
            hy_step, hz_step = hy, hz
        else:
            _, hy_prev, hz_prev = h_slab(x - 1, False, h_ref, hl_ref, hr_ref)
            hy_step, hz_step = hy - hy_prev, hz - hz_prev
        sig = sig_ref[x]
        quarter = 0.25 * sig
        eps = eps_ref[x]
        inv = 1.0 / (eps + quarter)
        scale_e = (eps - quarter) * inv
        scale_c = DT * inv
        ex0, ey0, ez0 = e_slab(x, first, e_ref, el_ref, er_ref)
        ex = scale_e * ex0 + scale_c * (bwd_y(hz) - bwd_z(hy))
        ey = scale_e * ey0 + scale_c * (bwd_z(hx) - hz_step)
        ez = scale_e * ez0 + scale_c * (hy_step - bwd_y(hx))
        out_ref[0, x] = ex
        out_ref[1, x] = ey
        out_ref[2, x] = ez
        at = pl.ds(x, 1)
        rows_ref[0, at, :] = ex[0:1]
        rows_ref[1, at, :] = ez[0:1]
        rows_ref[2, at, :] = scale_c[0:1]
        if first:
            layer_ref[0] = ey
            layer_ref[1] = ez
            layer_ref[2] = scale_c
        if final:
            before = ex0 * ex0 + ey0 * ey0 + ez0 * ez0
            half = 0.5 * sig
            refs[8][x] = half * (before + (ex * ex + ey * ey + ez * ez))
            rows_ref[3, at, :] = ey[0:1]
            rows_ref[4, at, :] = before[0:1]
            rows_ref[5, at, :] = half[0:1]
            if first:
                layer_ref[3] = ex
                layer_ref[4] = before
                layer_ref[5] = half

    walk(slab, nx, move)


def e_update(efield, e_fix, hfield, h_fix, eps, sig, final):
    _, nx, ny, nz = efield.shape
    args = [efield, *e_fix, hfield, *h_fix, eps, sig]
    kept = 6 if final else 3
    outs = [f32(3, nx, ny, nz), f32(kept, ny, nz), f32(kept, nx, nz)]
    specs = dense(3)
    scratch = []
    if final:
        outs[0] = hbm(3, nx, ny, nz)
        outs.append(f32(nx, ny, nz))
        specs = [hbm_spec(), vmem_spec(), vmem_spec(), vmem_spec()]
        scratch = [pltpu.VMEM((3, nx, ny, nz), jnp.float32), pltpu.SemaphoreType.DMA((copy_count(nx),))]
    return pl.pallas_call(
        functools.partial(e_kernel, bool(e_fix), final),
        in_specs=dense(len(args)),
        out_specs=specs,
        out_shape=outs,
        scratch_shapes=scratch,
        compiler_params=limit(16),
        cost_estimate=cost(60 * nx * ny * nz, 11 * MIB),
        name="estep",
    )(*args)


def e_border_values(layer_ref, rows_ref, gx_ref, gy_ref):
    ey_layer = layer_ref[0] + layer_ref[2] * gx_ref[1]
    ez_layer = layer_ref[1] - layer_ref[2] * gx_ref[0]
    ez_layer = patch_first(ez_layer, ez_layer[0:1] + layer_ref[2, 0:1] * gy_ref[0, 0:1])
    ex_rows = rows_ref[0] - rows_ref[2] * gy_ref[1]
    ez_rows = patch_first(rows_ref[1] + rows_ref[2] * gy_ref[0], ez_layer[0:1])
    return ey_layer, ez_layer, ex_rows, ez_rows


def e_border_kernel(layer_ref, rows_ref, gx_ref, gy_ref, layer_out, rows_out):
    layer_out[0], layer_out[1], rows_out[0], rows_out[1] = e_border_values(
        layer_ref, rows_ref, gx_ref, gy_ref
    )


def e_border(layer, rows, gx, gy):
    return pl.pallas_call(
        e_border_kernel,
        in_specs=dense(4),
        out_specs=dense(2),
        out_shape=[f32(*gx.shape), f32(*gy.shape)],
        compiler_params=limit(2),
        name="eborder",
    )(layer, rows, gx, gy)


def power_kernel(dest, p_ref, layer_ref, rows_ref, gx_ref, gy_ref, out_hbm, layer_out, rows_out, scratch, out_ref, sem):
    nx, ny, nz = p_ref.shape
    parts = ny // 8
    ey_layer, ez_layer, ex_rows, ez_rows = e_border_values(layer_ref, rows_ref, gx_ref, gy_ref)
    layer_out[0], layer_out[1], rows_out[0], rows_out[1] = ey_layer, ez_layer, ex_rows, ez_rows
    ex_layer = patch_first(layer_ref[3], ex_rows[0:1])
    squares = ex_layer * ex_layer + ey_layer * ey_layer + ez_layer * ez_layer
    layer_power = layer_ref[5] * (layer_ref[4] + squares)
    ey_rows = rows_ref[3]
    squares = ex_rows * ex_rows + ey_rows * ey_rows + ez_rows * ez_rows
    scratch[...] = rows_ref[5] * (rows_ref[4] + squares)
    top = lax.broadcasted_iota(jnp.int32, (8, nz), 0) == 0

    for part in range(parts):
        out_ref[dest[0, part]] = layer_power[part * 8 : part * 8 + 8]

    def body(x, carry):
        row = scratch[pl.ds(x, 1), :]
        out_ref[dest[0, x * parts]] = jnp.where(top, row, p_ref[x, 0:8, :])
        for part in range(1, parts):
            out_ref[dest[0, x * parts + part]] = p_ref[x, part * 8 : part * 8 + 8, :]
        return carry

    lax.fori_loop(1, nx, body, 0, unroll=8)
    move = pltpu.make_async_copy(out_ref, out_hbm, sem)
    move.start()
    move.wait()


def power_border(dest, power, layer, rows, gx, gy):
    nx, ny, nz = power.shape
    return pl.pallas_call(
        power_kernel,
        in_specs=[smem_spec()] + dense(5),
        out_specs=[hbm_spec()] + dense(2),
        out_shape=[hbm(nx * ny // 8, 8, nz), f32(*gx.shape), f32(*gy.shape)],
        scratch_shapes=[
            pltpu.VMEM((nx, nz), jnp.float32),
            pltpu.VMEM((nx * ny // 8, 8, nz), jnp.float32),
            pltpu.SemaphoreType.DMA(()),
        ],
        compiler_params=limit(8),
        cost_estimate=cost(4 * nx * ny * nz, 2 * MIB),
        name="power",
    )(dest, power, layer, rows, gx, gy)


def flush_kernel(e_ref, el_ref, er_ref, h_ref, hl_ref, hr_ref, e_out, h_out):
    nx = e_ref.shape[1]

    def slab(x, first, last):
        e_out[0, x], e_out[1, x], e_out[2, x] = e_slab(x, first, e_ref, el_ref, er_ref)
        h_out[0, x], h_out[1, x], h_out[2, x] = h_slab(x, last, h_ref, hl_ref, hr_ref)

    slab(0, True, False)
    lax.fori_loop(1, nx - 1, lambda x, c: (slab(x, False, False), c)[1], 0)
    slab(nx - 1, False, True)


def flush(efield, e_fix, hfield, h_fix):
    return pl.pallas_call(
        flush_kernel,
        in_specs=dense(6),
        out_specs=dense(2),
        out_shape=[f32(*efield.shape), f32(*hfield.shape)],
        compiler_params=limit(16),
        cost_estimate=cost(efield.size, 12 * MIB),
        name="flush",
    )(efield, *e_fix, hfield, *h_fix)


def pack_kernel(arrive, lines, t_ref, w_ref, c_ref, *out_refs):
    rows = out_refs[0].shape[0]
    width, nz = t_ref.shape[1:]
    levels = lines.shape[1]
    step = pl.program_id(0)
    lane = lax.broadcasted_iota(jnp.int32, (width, nz), 1)

    def body(r, carry):
        slot = arrive[0, step * rows + r]
        state = t_ref[slot]
        choice = c_ref[slot]
        above = jnp.where(lane == nz - 1, state, pltpu.roll(state, nz - 1, 1))
        below = jnp.where(lane == 0, state, pltpu.roll(state, 1, 1))
        factors = [jnp.full(choice.shape, lines[c, 0], jnp.float32) for c in range(4)]
        for level in range(1, levels):
            match = choice == level
            for c in range(4):
                factors[c] = jnp.where(match, lines[c, level], factors[c])
        wet = w_ref[slot]
        values = [
            state + 0.2 * ((above - state) + (below - state)),
            1.0 + factors[0],
            4.0 * factors[1] * wet,
            0.1 * factors[2],
            0.3 * factors[3] * wet,
        ]
        for k, value in enumerate(values):
            target, at = (out_refs[0], k) if k < FAR else (out_refs[1], k - FAR)
            target[r, at * width : (at + 1) * width, :] = value
        return carry

    lax.fori_loop(0, rows, body, 0, unroll=2)


def pack(arrive, lines, state, wetness, choice):
    n, width, nz = state.shape
    steps = 4
    return pl.pallas_call(
        pack_kernel,
        grid=(steps,),
        in_specs=[smem_spec(), smem_spec()] + dense(3),
        out_specs=[
            pl.BlockSpec((n // steps, count * width, nz), lambda i: (i, 0, 0))
            for count in (FAR, 5 - FAR)
            if count
        ],
        out_shape=[hbm(n, FAR * width, nz)] + [f32(n, (5 - FAR) * width, nz)] * (FAR < 5),
        compiler_params=limit(6),
        cost_estimate=cost(80 * n * width * nz, 9 * MIB),
        name="pack",
    )(arrive, lines, state, wetness, choice)


def thermal_kernel(p_hbm, far_hbm, *refs):
    near_refs, (send_hbm, p_ref, far_ref, send_ref, in_sem, out_sem) = refs[:-6], refs[-6:]
    n, width, nz = p_ref.shape
    chunks = in_sem.shape[1]
    size = n // chunks
    loads = copies([p_hbm, far_hbm], [p_ref, far_ref], in_sem, chunks)
    stores = copies([send_ref], [send_hbm], out_sem, chunks)
    for group in loads:
        for move in group:
            move.start()

    def body(s, carry):
        kept = [far_ref[s, k * width : (k + 1) * width, :] for k in range(FAR)]
        kept += [near_refs[0][s, k * width : (k + 1) * width, :] for k in range(5 - FAR)]
        heated = kept[0] + 0.5 * p_ref[s]
        share = jnp.exp(-2.0 * jnp.maximum(heated - 1.0, 0.0))
        send_ref[s, 0:width, :] = kept[1] + kept[2] * share
        send_ref[s, width : 2 * width, :] = kept[3] + kept[4] * share
        return carry

    for chunk in range(chunks):
        for move in loads[chunk]:
            move.wait()
        lax.fori_loop(chunk * size, (chunk + 1) * size, body, 0, unroll=16)
        for move in stores[chunk]:
            move.start()
    for group in stores:
        for move in group:
            move.wait()


def thermal(power, far, *near):
    n, width, nz = power.shape
    chunks = 8
    return pl.pallas_call(
        thermal_kernel,
        in_specs=[hbm_spec(), hbm_spec()] + dense(len(near)),
        out_specs=hbm_spec(),
        out_shape=hbm(n, 2 * width, nz),
        scratch_shapes=[
            pltpu.VMEM((n, width, nz), jnp.float32),
            pltpu.VMEM(far.shape, jnp.float32),
            pltpu.VMEM((n, 2 * width, nz), jnp.float32),
            pltpu.SemaphoreType.DMA((2, chunks)),
            pltpu.SemaphoreType.DMA((1, chunks)),
        ],
        compiler_params=limit(THERMAL_MIB),
        cost_estimate=cost(40 * n * width * nz, 8 * MIB),
        name="thermal",
    )(power, far, *near)


def heat_kernel(arrive, p_ref, t_ref, w_ref, t_out, w_out):
    n, width, nz = p_ref.shape
    lane = lax.broadcasted_iota(jnp.int32, (width, nz), 1)

    def body(s, carry):
        slot = arrive[0, s]
        state = t_ref[slot]
        above = jnp.where(lane == nz - 1, state, pltpu.roll(state, nz - 1, 1))
        below = jnp.where(lane == 0, state, pltpu.roll(state, 1, 1))
        heated = state + 0.2 * ((above - state) + (below - state)) + 0.5 * p_ref[s]
        wet = w_ref[slot]
        gone = wet * (1.0 - jnp.exp(-2.0 * jnp.maximum(heated - 1.0, 0.0)))
        w_out[slot] = wet - gone
        t_out[slot] = heated - 0.8 * gone
        return carry

    lax.fori_loop(0, n, body, 0, unroll=4)


def heat(arrive, power, state, wetness):
    n, width, nz = power.shape
    return pl.pallas_call(
        heat_kernel,
        in_specs=[smem_spec()] + dense(3),
        out_specs=dense(2),
        out_shape=[f32(n, width, nz)] * 2,
        compiler_params=limit(8),
        cost_estimate=cost(40 * n * width * nz, 5 * MIB),
        name="heat",
    )(arrive, power, state, wetness)


def near_kernel(eps_ref, sig_ref, lab_ref, out_ref):
    out_ref[0] = jnp.where(lab_ref[...] == 2, -1.0, eps_ref[...])
    out_ref[1] = sig_ref[...]


def near(eps, sig, label):
    nx, ny, nz = eps.shape
    steps = 4
    cells = pl.BlockSpec((nx // steps, ny, nz), lambda i: (i, 0, 0))
    return pl.pallas_call(
        near_kernel,
        grid=(steps,),
        in_specs=[cells] * 3,
        out_specs=pl.BlockSpec((2, nx // steps, ny, nz), lambda i: (0, i, 0, 0)),
        out_shape=f32(2, nx, ny, nz),
        compiler_params=limit(4),
        cost_estimate=cost(2 * nx * ny * nz, 5 * MIB),
        name="near",
    )(eps, sig, label)


def select_kernel(dest, recv_hbm, kept, eps_out, sig_out, recv, eps_new, sig_new, recv_sem, out_sem):
    nx, ny, nz = eps_new.shape
    parts = ny // 8
    chunks = out_sem.shape[1]
    size = nx // chunks
    group = size * parts
    stores = copies([eps_new, sig_new], [eps_out, sig_out], out_sem, chunks)

    for chunk in range(chunks):

        def fetch(k, carry, chunk=chunk):
            pltpu.make_async_copy(recv_hbm.at[dest[0, k]], recv.at[k], recv_sem.at[chunk]).start()
            return carry

        lax.fori_loop(chunk * group, (chunk + 1) * group, fetch, 0, unroll=16)

    def body(x, carry):
        for part in range(parts):
            rows = slice(part * 8, part * 8 + 8)
            eps = kept[0, x, rows, :]
            product = eps < 0.0
            eps_new[x, rows, :] = jnp.where(product, recv[x * parts + part, 0:8, :], eps)
            sig_new[x, rows, :] = jnp.where(product, recv[x * parts + part, 8:16, :], kept[1, x, rows, :])
        return carry

    for chunk in range(chunks):
        block = pl.ds(chunk * group, group)
        pltpu.make_async_copy(recv_hbm.at[block], recv.at[block], recv_sem.at[chunk]).wait()
        lax.fori_loop(chunk * size, (chunk + 1) * size, body, 0, unroll=4)
        for move in stores[chunk]:
            move.start()
    for moves in stores:
        for move in moves:
            move.wait()


def select(dest, recv, kept):
    nx, ny, nz = kept.shape[1:]
    chunks = 8
    cells = pltpu.VMEM((nx, ny, nz), jnp.float32)
    return pl.pallas_call(
        select_kernel,
        in_specs=[smem_spec(), hbm_spec(), vmem_spec()],
        out_specs=[hbm_spec()] * 2,
        out_shape=[hbm(nx, ny, nz), hbm(nx, ny, nz)],
        scratch_shapes=[
            pltpu.VMEM(recv.shape, jnp.float32),
            cells,
            cells,
            pltpu.SemaphoreType.DMA((chunks,)),
            pltpu.SemaphoreType.DMA((2, chunks)),
        ],
        compiler_params=limit(8),
        cost_estimate=cost(4 * nx * ny * nz, 7 * MIB),
        name="select",
    )(dest, recv, kept)


def exchange(value):
    return lax.all_to_all(value, ("gx", "gy"), split_axis=0, concat_axis=0, tiled=True)


def borders(layer, rows, by):
    return passed_along(layer, "gx", by), passed_along(rows, "gy", by)


def local(
    efield_vector,
    hfield_vector,
    dielectric_grid,
    sigma_grid,
    substance_label,
    thermal_state,
    wetness_share,
    dielectric_line_choice,
    dielectric_lookup_lines,
    dispatch_keeper_map,
    arrival_position_map,
):
    efield, hfield = efield_vector, hfield_vector
    e_fix, h_fix = (), ()
    layer, rows = first_halo(efield)
    for step in range(2):
        gx, gy = borders(layer, rows, -1)
        hfield, layer, rows, *h_kept = h_update(efield, e_fix, hfield, h_fix)
        h_fix = h_border(layer, rows, gx, gy)
        gx, gy = borders(*h_fix, 1)
        final = step == 1
        efield, layer, rows, *power = e_update(
            efield, e_fix, hfield, h_fix, dielectric_grid, sigma_grid, final
        )
        if final:
            power, *e_fix = power_border(dispatch_keeper_map, power[0], layer, rows, gx, gy)
        else:
            e_fix = layer, rows = e_border(layer, rows, gx, gy)
    arrived = exchange(power)
    blocks = lax.optimization_barrier(
        (power, thermal_state, wetness_share, dielectric_line_choice)
    )
    packed = pack(arrival_position_map, dielectric_lookup_lines, *blocks[1:])
    outgoing = thermal(arrived, *packed)
    returned = exchange(outgoing)
    outgoing, arrived, efield, hfield, label = lax.optimization_barrier(
        (outgoing, arrived, efield, h_kept[0], substance_label)
    )
    kept = near(dielectric_grid, sigma_grid, label)
    final_efield, final_hfield = flush(efield, e_fix, hfield, h_fix)
    warmth, moisture = heat(arrival_position_map, arrived, thermal_state, wetness_share)
    dielectric_result, sigma_result = select(
        dispatch_keeper_map, returned, kept
    )
    return final_efield, final_hfield, dielectric_result, sigma_result, warmth, moisture


def solution(mesh):
    in_specs = (
        P(None, "gx", "gy", None),
        P(None, "gx", "gy", None),
        P("gx", "gy", None),
        P("gx", "gy", None),
        P("gx", "gy", None),
        P(("gx", "gy"), None, None),
        P(("gx", "gy"), None, None),
        P(("gx", "gy"), None, None),
        P(),
        P(("gx", "gy"), None),
        P(("gx", "gy"), None),
    )
    out_specs = (
        P(None, "gx", "gy", None),
        P(None, "gx", "gy", None),
        P("gx", "gy", None),
        P("gx", "gy", None),
        P(("gx", "gy"), None, None),
        P(("gx", "gy"), None, None),
    )
    return jax.shard_map(local, mesh=mesh, in_specs=in_specs, out_specs=out_specs, check_vma=False)
```
